32 devices in a mesh: groups: 2 (over x), space: 16 (over z, y, core).
Axes of the slice: x: 2, y: 2, z: 4, core: 2. Of those that a mesh axis runs over, the one named last changes fastest.
Arguments:
- lifted_field: float32 [64, 16, 128, 256], P('groups', 'space'), parts along dimension 0, may hold values from -6 to 6
- cotangent: bfloat16 [64, 16, 128, 256], P('groups', 'space'), parts along dimension 0, may hold values from -6 to 6
- spectral_weights: float32 [2, 32, 1024, 32, 32], P(None, None, 'space'), may hold values from -4 to 4
- point_weights: float32 [32, 32], replicated, may hold values from -1 to 1
- point_bias: float32 [32], replicated, may hold values from -3 to 3
Outputs:
- activated: bfloat16 [64, 16, 128, 256], P('groups', 'space'), parts along dimension 0
- grad_spectral: float32 [4, 32, 1024, 32, 32], P('groups', None, 'space'), parts along dimension 0
- grad_point: float32 [64, 32], P('groups'), parts along dimension 0
- grad_bias: float32 [64], P('groups'), parts along dimension 0
The draws below stay inside these ranges and needn't reach their ends.
There are 2 independent parts, one for each index of `groups`. The reference program is written for one: setup_inputs(seed, part) draws one part's arguments, and reference() takes and returns one part's arrays. A program takes and returns all parts, laid end to end along the dimension named above; an argument that names none is the same for every part. Nothing has to cross between parts.
All inputs are finite; a program needn't handle non-finite values.
Results may differ from the reference program's by a relative error of at most 0.001.
Values sent between devices are 32-bit elements; how exact they have to be, the bound alone decides.
A program may use at most 192 MiB of HBM per device.

```python
import jax
import jax.numpy as jnp
from jax import lax

C = 32
MX = 32
MY = 32
MZ = 32
NY = 128
NZ = 256
NX = 16
MODES = 1024


def block_levels(own_key, shape, split, smallest, top_value):
    level = 1.0
    for axis_at, shards_of in split:
        steps = jax.random.uniform(jax.random.fold_in(jax.random.fold_in(own_key, 6), axis_at), (shards_of,), jnp.float32, smallest / len(split), top_value / len(split))
        level = level * jnp.repeat(jnp.exp(steps), shape[axis_at] // shards_of).reshape((-1,) + (1,) * (len(shape) - 1 - axis_at))
    return level


def centred(stream_key, extent, scale, most, split=(), kind=jnp.bfloat16):
    loudness = block_levels(stream_key, extent, split, -0.22, 0.18) if split else 1.0
    values = jax.random.normal(stream_key, extent, jnp.float32) * scale * loudness
    return jnp.minimum(jnp.maximum(values, -most), most).astype(kind)


def setup_inputs(seed: int = 0, part: int = 0) -> dict:
    streams_of = jax.random.split(jax.random.key(seed), 6)
    part_keys = jax.random.split(jax.random.fold_in(streams_of[5], part), 6)
    lifted_field = centred(part_keys[0], (C, NX, NY, NZ), 1.0, 6.0, ((1, 16),), jnp.float32)
    cotangent = centred(part_keys[1], (C, NX, NY, NZ), 1.0, 6.0, ((1, 16),))
    spectral_weights = centred(streams_of[2], (2, MX, MODES, C, C), (C // 16) ** -0.5, 4.0, ((2, 16),), jnp.float32)
    point_weights = centred(streams_of[3], (C, C), C ** -0.5, 1.0, (), jnp.float32)
    point_bias = centred(streams_of[4], (C,), 0.5, 3.0, (), jnp.float32)
    return {"lifted_field": lifted_field, "cotangent": cotangent, "spectral_weights": spectral_weights, "point_weights": point_weights, "point_bias": point_bias}


HIGHEST = lax.Precision.HIGHEST
INV_SQRT_TWO = 0.7071067811865476
INV_SQRT_TWO_PI = 0.3989422804014327


def trig_tables(positions, frequency, length):
    product = (positions[:, None] * frequency[None, :]) % length
    phase_angle = (2.0 * jnp.pi / length) * product.astype(jnp.float32)
    return jnp.cos(phase_angle), jnp.sin(phase_angle)


def kept_frequencies(kept_count, length):
    mode_index = jnp.arange(kept_count, dtype=jnp.int32)
    return jnp.where(mode_index < kept_count // 2, mode_index, length - kept_count + mode_index).astype(jnp.int32)


def forward_local(field_in):
    channels = field_in.shape[0]
    width_x = field_in.shape[1]
    cos_z, sin_z = trig_tables(jnp.arange(NZ, dtype=jnp.int32), jnp.arange(MZ, dtype=jnp.int32), NZ)
    table_z = jnp.concatenate([cos_z, -sin_z], axis=1)
    along_z = jnp.einsum("cxyz,zk->cxyk", field_in, table_z, precision=HIGHEST)
    z_real = along_z[..., :MZ]
    z_imag = along_z[..., MZ:]
    cos_y, sin_y = trig_tables(jnp.arange(NY, dtype=jnp.int32), kept_frequencies(MY, NY), NY)
    y_real = jnp.einsum("cxyk,yj->xcjk", z_real, cos_y, precision=HIGHEST) + jnp.einsum("cxyk,yj->xcjk", z_imag, sin_y, precision=HIGHEST)
    y_imag = jnp.einsum("cxyk,yj->xcjk", z_imag, cos_y, precision=HIGHEST) - jnp.einsum("cxyk,yj->xcjk", z_real, sin_y, precision=HIGHEST)
    stacked = jnp.stack([y_real, y_imag], axis=1)
    return stacked.reshape(width_x, 2, channels, MY * MZ)


def transform_x(x_lines):
    length_x = x_lines.shape[0]
    cos_x, sin_x = trig_tables(jnp.arange(length_x, dtype=jnp.int32), kept_frequencies(MX, length_x), length_x)
    norm_scale = 1.0 / (float(length_x * NY * NZ) ** 0.5)
    part_real = x_lines[:, 0]
    part_imag = x_lines[:, 1]
    x_real = jnp.einsum("xcm,xk->kcm", part_real, cos_x, precision=HIGHEST) + jnp.einsum("xcm,xk->kcm", part_imag, sin_x, precision=HIGHEST)
    x_imag = jnp.einsum("xcm,xk->kcm", part_imag, cos_x, precision=HIGHEST) - jnp.einsum("xcm,xk->kcm", part_real, sin_x, precision=HIGHEST)
    return norm_scale * jnp.stack([x_real, x_imag], axis=1)


def mix_modes(spectrum, weights):
    spec_real = spectrum[:, 0]
    spec_imag = spectrum[:, 1]
    out_real = jnp.einsum("kim,kmio->kom", spec_real, weights[0], precision=HIGHEST) - jnp.einsum("kim,kmio->kom", spec_imag, weights[1], precision=HIGHEST)
    out_imag = jnp.einsum("kim,kmio->kom", spec_real, weights[1], precision=HIGHEST) + jnp.einsum("kim,kmio->kom", spec_imag, weights[0], precision=HIGHEST)
    return jnp.stack([out_real, out_imag], axis=1)


def inverse_x(spectrum, positions, length_x):
    cos_x, sin_x = trig_tables(positions, kept_frequencies(MX, length_x), length_x)
    spec_real = spectrum[:, 0]
    spec_imag = spectrum[:, 1]
    a_real = jnp.einsum("kcm,xk->xcm", spec_real, cos_x, precision=HIGHEST) - jnp.einsum("kcm,xk->xcm", spec_imag, sin_x, precision=HIGHEST)
    a_imag = jnp.einsum("kcm,xk->xcm", spec_imag, cos_x, precision=HIGHEST) + jnp.einsum("kcm,xk->xcm", spec_real, sin_x, precision=HIGHEST)
    return jnp.stack([a_real, a_imag], axis=1)


def inverse_yz(x_lines, length_x):
    width_x = x_lines.shape[0]
    channels = x_lines.shape[2]
    mode_grid = x_lines.reshape(width_x, 2, channels, MY, MZ)
    cos_y, sin_y = trig_tables(jnp.arange(NY, dtype=jnp.int32), kept_frequencies(MY, NY), NY)
    b_real = jnp.einsum("xcjk,yj->cxyk", mode_grid[:, 0], cos_y, precision=HIGHEST) - jnp.einsum("xcjk,yj->cxyk", mode_grid[:, 1], sin_y, precision=HIGHEST)
    b_imag = jnp.einsum("xcjk,yj->cxyk", mode_grid[:, 1], cos_y, precision=HIGHEST) + jnp.einsum("xcjk,yj->cxyk", mode_grid[:, 0], sin_y, precision=HIGHEST)
    cos_z, sin_z = trig_tables(jnp.arange(NZ, dtype=jnp.int32), jnp.arange(MZ, dtype=jnp.int32), NZ)
    weight_z = jnp.where(jnp.arange(MZ, dtype=jnp.int32) == 0, 1.0, 2.0).astype(jnp.float32)
    table_z = jnp.concatenate([cos_z * weight_z[None, :], -sin_z * weight_z[None, :]], axis=1)
    stacked = jnp.concatenate([b_real, b_imag], axis=-1)
    result = jnp.einsum("cxyk,zk->cxyz", stacked, table_z, precision=HIGHEST)
    return result * (1.0 / (float(length_x * NY * NZ) ** 0.5))


def gelu_slope(values):
    return 0.5 * (1.0 + lax.erf(values * INV_SQRT_TWO)) + values * jnp.exp(-0.5 * values * values) * INV_SQRT_TWO_PI


def weight_gradient(spectrum, slope_modes, first_mode):
    mode_ids = first_mode + jnp.arange(spectrum.shape[3], dtype=jnp.int32)
    weight_modes = jnp.where(mode_ids % MZ == 0, 1.0, 2.0).astype(jnp.float32)
    grad_real = jnp.einsum("kim,kom->kmio", spectrum[:, 0], slope_modes[:, 0], precision=HIGHEST) + jnp.einsum("kim,kom->kmio", spectrum[:, 1], slope_modes[:, 1], precision=HIGHEST)
    grad_imag = jnp.einsum("kim,kom->kmio", spectrum[:, 0], slope_modes[:, 1], precision=HIGHEST) - jnp.einsum("kim,kom->kmio", spectrum[:, 1], slope_modes[:, 0], precision=HIGHEST)
    stacked = jnp.stack([grad_real, grad_imag], axis=0)
    return stacked * weight_modes[None, None, :, None, None]


def reference(lifted_field, cotangent, spectral_weights, point_weights, point_bias):
    length_x = lifted_field.shape[1]
    spectrum = transform_x(forward_local(lifted_field))
    mixed_modes = mix_modes(spectrum, spectral_weights)
    x_lines = inverse_x(mixed_modes, jnp.arange(length_x, dtype=jnp.int32), length_x)
    spectral = inverse_yz(x_lines, length_x)
    pointwise = jnp.einsum("ixyz,io->oxyz", lifted_field, point_weights, precision=HIGHEST) + point_bias[:, None, None, None]
    before = spectral + pointwise
    activated = jax.nn.gelu(before, approximate=False).astype(jnp.bfloat16)
    slope_field = cotangent.astype(jnp.float32) * gelu_slope(before)
    root_cells = float(length_x * NY * NZ) ** 0.5
    grad_point = jnp.einsum("ixyz,oxyz->io", lifted_field, slope_field, precision=HIGHEST) / root_cells
    grad_bias = jnp.sum(slope_field, axis=(1, 2, 3)) / root_cells
    slope_spectrum = transform_x(forward_local(slope_field))
    grad_spectral = weight_gradient(spectrum, slope_spectrum, jnp.int32(0))
    return (activated, grad_spectral, grad_point, grad_bias)
```

```python
import functools

import jax
import jax.numpy as jnp
import numpy as np
from jax import lax
from jax.experimental import pallas as pl
from jax.experimental.pallas import tpu as pltpu
from jax.sharding import PartitionSpec as P

MX = 32
MY = 32
MZ = 32
ROWS = 8
STEP = 32

HIGH = lax.Precision.HIGH
INV_SQRT_TWO = 0.7071067811865476
INV_SQRT_TWO_PI = 0.3989422804014327


def angles(positions, frequency, length):
    product = np.outer(np.asarray(positions), np.asarray(frequency)) % length
    phase = 2.0 * np.pi / length * product.astype(np.float64)
    return np.cos(phase), np.sin(phase)


def kept(count, length):
    index = np.arange(count)
    return np.where(index < count // 2, index, length - count + index)


def halves(table):
    table = np.asarray(table, np.float32)
    high = table.astype(jnp.bfloat16)
    low = (table - high.astype(np.float32)).astype(jnp.bfloat16)
    return jnp.asarray(high), jnp.asarray(low)


def split(value):
    high = value.astype(jnp.bfloat16)
    low = (value - high.astype(jnp.float32)).astype(jnp.bfloat16)
    return high, low


def dot3(a, b, dims=(((1,), (0,)), ((), ()))):
    one = functools.partial(
        lax.dot_general, dimension_numbers=dims, preferred_element_type=jnp.float32
    )
    return one(a[0], b[0]) + (one(a[0], b[1]) + one(a[1], b[0]))


def forward_tables(ny, nz):
    cos_z, sin_z = angles(np.arange(nz), np.arange(MZ), nz)
    table_z = np.concatenate([cos_z, -sin_z, -sin_z, -cos_z], axis=1)
    cos_y, sin_y = angles(np.arange(ny), kept(MY, ny), ny)
    table_y = np.concatenate([cos_y.T, sin_y.T], axis=0)
    return halves(table_z) + halves(table_y)


def inverse_tables(ny, nz, scale, local_rows):
    cos_z, sin_z = angles(np.arange(nz), np.arange(MZ), nz)
    weight = np.where(np.arange(MZ) == 0, 1.0, 2.0)[:, None] * scale
    real = np.kron(np.eye(4), cos_z.T * weight)
    imag = np.kron(np.eye(4), -sin_z.T * weight)
    cos_y, sin_y = angles(np.arange(ny), kept(MY, ny), ny)
    if local_rows is None:
        cos_y = np.concatenate([cos_y[:, 0::2], cos_y[:, 1::2]], axis=1)
        sin_y = np.concatenate([sin_y[:, 0::2], sin_y[:, 1::2]], axis=1)
        real_y = np.concatenate([cos_y, -sin_y], axis=1)
        imag_y = np.concatenate([sin_y, cos_y], axis=1)
    else:
        cos_y = cos_y.reshape(ny, MY // local_rows, local_rows)
        sin_y = sin_y.reshape(ny, MY // local_rows, local_rows)
        real_y = np.stack([cos_y, -sin_y], 2).reshape(ny, 2 * MY)
        imag_y = np.stack([sin_y, cos_y], 2).reshape(ny, 2 * MY)
    return halves(np.concatenate([real, imag], 0)) + halves(np.concatenate([real_y, imag_y], 0))


def finish_y(lines, ty, modes_ref):
    def one(c, carry):
        both = dot3(ty, split(lines[c]))
        turned = pltpu.roll(both[MY:], 2 * MZ, 1)
        modes_ref[c] = (both[:MY] + turned)[:, : 2 * MZ]
        return carry

    lax.fori_loop(0, lines.shape[0], one, 0, unroll=16)


def forward_kernel(x_ref, tzh, tzl, tyh, tyl, modes_ref, lines):
    step = pl.program_id(1)
    channels, rows, nz = x_ref.shape
    value = x_ref[...].reshape(channels * rows, nz)
    along = dot3(split(value), (tzh[...], tzl[...]))
    start = pl.multiple_of(step * rows, rows)
    lines[:, pl.ds(start, rows), :] = along.reshape(channels, rows, 4 * MZ)

    @pl.when(step == pl.num_programs(1) - 1)
    def _():
        finish_y(lines, (tyh[...], tyl[...]), modes_ref)


def whole(array):
    shape = array.shape
    return pl.BlockSpec(shape, lambda *_: (0,) * len(shape))


def field_spec(channels, nz):
    return pl.BlockSpec((channels, None, STEP, nz), lambda x, y: (0, x, y, 0))


def modes_spec(channels):
    return pl.BlockSpec((None, channels, MY, 2 * MZ), lambda x, y: (x, 0, 0, 0))


def forward_modes(field):
    channels, width, ny, nz = field.shape
    tables = forward_tables(ny, nz)
    return pl.pallas_call(
        forward_kernel,
        grid=(width, ny // STEP),
        out_shape=jax.ShapeDtypeStruct((width, channels, MY, 2 * MZ), jnp.float32),
        in_specs=[field_spec(channels, nz)] + [whole(t) for t in tables],
        out_specs=modes_spec(channels),
        scratch_shapes=[pltpu.VMEM((channels, ny, 4 * MZ), jnp.float32)],
        name="forward_modes",
    )(field, *tables)


def middle_kernel(
    m_ref, x_ref, cot_ref, w_ref, bias_ref, pick, bdh, bdl, iyh, iyl, tzh, tzl, tyh, tyl,
    act_ref, modes_ref, point_ref, lines, inverse, field_part, wh, wl, total,
):
    step = pl.program_id(1)
    channels, rows, nz = x_ref.shape
    quads = channels // 4
    width = 4 * MZ
    ny = lines.shape[1]

    def same_row():
        size = channels * ROWS
        row = lax.broadcasted_iota(jnp.int32, (size, size), 0) % ROWS
        column = lax.broadcasted_iota(jnp.int32, (size, size), 1) % ROWS
        return row == column

    @pl.when(step == 0)
    def _():
        for part in range(0, m_ref.shape[1], 256):
            lanes = pl.ds(part, 256)
            both = dot3((iyh[...], iyl[...]), split(m_ref[:, lanes]))
            inverse[0, :, lanes] = both[:ny]
            inverse[1, :, lanes] = both[ny:]
        contract = (((1,), (1,)), ((), ()))
        for narrow, out in zip(split(w_ref[...]), (wh, wl)):
            tall = lax.dot_general(
                pick[...], narrow, contract, preferred_element_type=jnp.float32
            ).astype(jnp.bfloat16)
            square = lax.dot_general(tall, pick[...], contract, preferred_element_type=jnp.float32)
            out[...] = jnp.where(same_row(), square, 0.0).astype(jnp.bfloat16)
        total[...] = jnp.zeros_like(total)

    first = pl.multiple_of(step * rows, rows)
    stacked = jnp.concatenate(
        [
            jnp.concatenate(
                [
                    inverse[r, pl.ds(first, rows), g * width : (g + 1) * width]
                    for r in range(2)
                ],
                axis=1,
            )
            for g in range(quads)
        ],
        axis=0,
    )
    stacked = split(stacked)
    for c in range(4):
        lanes = slice(c * nz, (c + 1) * nz)
        field_part[:, lanes] = dot3(stacked, (bdh[:, lanes], bdl[:, lanes]))

    for half in range(rows // ROWS):
        here = slice(half * ROWS, (half + 1) * ROWS)
        start = pl.multiple_of(step * rows + half * ROWS, ROWS)
        spectral = jnp.concatenate(
            [
                field_part[
                    g * rows + half * ROWS : g * rows + (half + 1) * ROWS, c * nz : (c + 1) * nz
                ]
                for g in range(quads)
                for c in range(4)
            ],
            axis=0,
        )
        field = split(x_ref[:, here, :].reshape(channels * ROWS, nz))
        before = spectral + dot3((wh[...], wl[...]), field)
        before = before.reshape(channels, ROWS, nz) + bias_ref[...]
        normal = 0.5 * (1.0 + lax.erf(before * INV_SQRT_TWO))
        density = jnp.exp(-0.5 * before * before) * INV_SQRT_TWO_PI
        act_ref[:, here, :] = (before * normal).astype(jnp.bfloat16)
        slope = cot_ref[:, here, :].astype(jnp.float32) * (normal + before * density)
        slope = split(slope.reshape(channels * ROWS, nz))
        total[...] += dot3(field, slope, (((1,), (1,)), ((), ())))
        along = dot3(slope, (tzh[...], tzl[...]))
        lines[:, pl.ds(start, ROWS), :] = along.reshape(channels, ROWS, 4 * MZ)

    @pl.when(step == pl.num_programs(1) - 1)
    def _():
        finish_y(lines, (tyh[...], tyl[...]), modes_ref)
        size = channels * ROWS
        diagonal = jnp.where(same_row(), total[...], 0.0)
        point_ref[...] = jnp.sum(diagonal.reshape(channels, ROWS, size), axis=1)


def middle(grid_modes, local_rows, field, cotangent, point_weights, point_bias, scale):
    channels, width, ny, nz = field.shape
    size = channels * ROWS
    tables = inverse_tables(ny, nz, scale, local_rows) + forward_tables(ny, nz)
    pick = jnp.asarray(np.repeat(np.eye(channels, dtype=np.float32), ROWS, 0).astype(jnp.bfloat16))
    bias = jnp.broadcast_to(point_bias[:, None, None], (channels, 1, nz))
    spec = field_spec(channels, nz)
    mixed_spec = pl.BlockSpec((None,) + grid_modes.shape[1:], lambda x, y: (x, 0, 0))
    return pl.pallas_call(
        middle_kernel,
        grid=(width, ny // STEP),
        out_shape=(
            jax.ShapeDtypeStruct(field.shape, jnp.bfloat16),
            jax.ShapeDtypeStruct((width, channels, MY, 2 * MZ), jnp.float32),
            jax.ShapeDtypeStruct((width, channels, size), jnp.float32),
        ),
        in_specs=[mixed_spec, spec, spec, whole(point_weights), whole(bias), whole(pick)]
        + [whole(t) for t in tables],
        out_specs=(
            spec,
            modes_spec(channels),
            pl.BlockSpec((None, channels, size), lambda x, y: (x, 0, 0)),
        ),
        scratch_shapes=[
            pltpu.VMEM((channels, ny, 4 * MZ), jnp.float32),
            pltpu.VMEM((2, ny, channels * MZ), jnp.float32),
            pltpu.VMEM((channels // 4 * STEP, 4 * nz), jnp.float32),
            pltpu.VMEM((size, size), jnp.bfloat16),
            pltpu.VMEM((size, size), jnp.bfloat16),
            pltpu.VMEM((size, size), jnp.float32),
        ],
        name="middle",
    )(grid_modes, field, cotangent, point_weights, bias, pick, *tables)


def weight_gradient(spectrum, slope_modes):
    turned = jnp.stack([slope_modes[1], -slope_modes[0]], axis=0)
    slope_modes, turned = lax.optimization_barrier((slope_modes, turned))
    real = spectrum[0][None, :, :, None, :]
    imag = spectrum[1][None, :, :, None, :]
    out = real * slope_modes[:, :, None] + imag * turned[:, :, None]
    return out.transpose(0, 1, 4, 2, 3)


def packed_tables(ny, nz):
    cos_z, sin_z = angles(np.arange(nz), np.arange(MZ), nz)
    table_z = np.concatenate([cos_z, cos_z, -sin_z, -sin_z], axis=1)
    cos_y, sin_y = angles(np.arange(ny), kept(MY, ny), ny)
    cos_y, sin_y = cos_y.T, sin_y.T
    table_y = np.concatenate([cos_y[0::2], cos_y[1::2], sin_y[0::2], sin_y[1::2]], axis=0)
    return halves(table_z) + halves(table_y)


def lane_ids(rows):
    return lax.broadcasted_iota(jnp.int32, (rows, 4 * MZ), 1)


def turn(value):
    rolled = pltpu.roll(value, 2 * MZ, 1)
    return jnp.where(lane_ids(value.shape[0]) < 2 * MZ, rolled, -rolled)


def message_rows(ty, line):
    both = dot3(ty, split(line))
    count = MY // 2
    even = lane_ids(count) // MZ % 2 == 0
    cos_part = jnp.where(even, both[:count], both[count : 2 * count])
    sin_part = jnp.where(even, both[2 * count : 3 * count], both[3 * count :])
    return cos_part + turn(sin_part)


def along_x(parts, sign):
    length = len(parts)
    half = length // 2
    plus = [parts[x] + parts[length - x] for x in range(1, half)]
    minus = [turn(parts[x] - parts[length - x]) for x in range(1, half)]
    ends = (parts[0] + parts[half], parts[0] - parts[half])
    out = [None] * length
    for k in range(half + 1):
        even = ends[k % 2]
        odd = None
        for x in range(1, half):
            even = even + plus[x - 1] * float(np.cos(2 * np.pi * (k * x % length) / length))
            if 0 < k < half:
                term = minus[x - 1] * float(np.sin(2 * np.pi * (k * x % length) / length))
                odd = term if odd is None else odd + term
        if odd is None:
            out[k] = even
        else:
            out[k] = even + odd if sign > 0 else even - odd
            out[length - k] = even - odd if sign > 0 else even + odd
    return out


def greet_peers(devices):
    me = lax.axis_index("space")
    barrier = pltpu.get_barrier_semaphore()

    def greet(step, carry):
        pl.semaphore_signal(
            barrier,
            inc=1,
            device_id={"space": lax.rem(me + step, devices)},
            device_id_type=pl.DeviceIdType.MESH,
        )
        return carry

    lax.fori_loop(1, devices, greet, 0)


def meet_peers(devices):
    pl.semaphore_wait(pltpu.get_barrier_semaphore(), devices - 1)


def message(devices, channels, src, recv, sems, step, part, owner):
    me = lax.axis_index("space")
    peer = lax.rem(me + step, devices)
    there = pl.ds(pl.multiple_of(peer * channels + part * 8, 8), 8)
    here = pl.ds(pl.multiple_of(owner * channels + part * 8, 8), 8)
    return pltpu.make_async_remote_copy(
        src_ref=src.at[there],
        dst_ref=recv.at[here],
        send_sem=sems.at[0, part, step],
        recv_sem=sems.at[1, part, step],
        device_id={"space": peer},
        device_id_type=pl.DeviceIdType.MESH,
    )


def send_part(devices, channels, src, recv, sems, part):
    me = lax.axis_index("space")

    def send(step, carry):
        message(devices, channels, src, recv, sems, step, part, me).start()
        return carry

    lax.fori_loop(1, devices, send, 0)


def keep_own(channels, src, recv):
    me = lax.axis_index("space")
    own = pl.ds(pl.multiple_of(me * channels, channels), channels)
    recv[own, :] = src[own, :]


def take_part(devices, channels, src, recv, sems, part):
    me = lax.axis_index("space")

    def take(step, carry):
        owner = lax.rem(me + devices - step, devices)
        done = message(devices, channels, src, recv, sems, step, part, owner)
        done.wait_send()
        done.wait_recv()
        return carry

    lax.fori_loop(1, devices, take, 0)


def x_modes(devices, channels, scale, recv, part, real_ref, imag_ref):
    start = pl.multiple_of(part * 8, 8)
    parts = [recv[pl.ds(x * channels + start, 8), :] for x in range(devices)]
    for k, value in enumerate(along_x(parts, 1)):
        value = value * scale
        real, imag = value[:, : 2 * MZ], value[:, 2 * MZ :]
        for alias in range(k, real_ref.shape[0], devices):
            real_ref[alias, pl.ds(start, 8), :] = real
            imag_ref[alias, pl.ds(start, 8), :] = imag


def front_kernel(
    devices, channels, scale, x_ref, tzh, tzl, tyh, tyl, real_ref, imag_ref, lines, src, recv, sems
):
    part = pl.program_id(0)

    @pl.when(part == 0)
    def _():
        greet_peers(devices)

    rows, ny, nz = x_ref.shape
    value = x_ref[...].reshape(rows * ny, nz)
    along = dot3(split(value), (tzh[...], tzl[...]))
    lines[...] = along.reshape(rows, ny, 4 * MZ)
    ty = (tyh[...], tyl[...])
    for c in range(rows):
        src[pl.ds(part * rows + c, devices, stride=channels), :] = message_rows(ty, lines[c])

    @pl.when(part == 0)
    def _():
        meet_peers(devices)

    send_part(devices, channels, src, recv, sems, part)

    @pl.when(part == pl.num_programs(0) - 1)
    def _():
        keep_own(channels, src, recv)

        def finish(part, carry):
            take_part(devices, channels, src, recv, sems, part)
            x_modes(devices, channels, scale, recv, part, real_ref, imag_ref)
            return carry

        lax.fori_loop(0, channels // 8, finish, 0)


def front(field, devices, scale):
    channels, _, ny, nz = field.shape
    tables = packed_tables(ny, nz)
    parts = channels // 8
    spectrum = jax.ShapeDtypeStruct((MX, channels, 2 * MZ), jnp.float32)
    return pl.pallas_call(
        functools.partial(front_kernel, devices, channels, scale),
        grid=(parts,),
        out_shape=(spectrum, spectrum),
        in_specs=[pl.BlockSpec((8, None, ny, nz), lambda c: (c, 0, 0, 0))]
        + [whole(t) for t in tables],
        out_specs=(whole(spectrum), whole(spectrum)),
        scratch_shapes=[
            pltpu.VMEM((8, ny, 4 * MZ), jnp.float32),
            pltpu.VMEM((devices * channels, 4 * MZ), jnp.float32),
            pltpu.VMEM((devices * channels, 4 * MZ), jnp.float32),
            pltpu.SemaphoreType.DMA((2, parts, devices)),
        ],
        compiler_params=pltpu.CompilerParams(
            collective_id=0, has_side_effects=True, vmem_limit_bytes=14 * 2**20
        ),
        cost_estimate=pl.CostEstimate(flops=10**10, bytes_accessed=40 * 10**6, transcendentals=0),
        name="front",
    )(field, *tables)


def mix_kernel(devices, channels, real_ref, imag_ref, w_ref, out_ref, mixed, src, recv, sems):
    greet_peers(devices)
    local = real_ref.shape[2]
    aliases = range(0, real_ref.shape[0], devices)
    parts = channels // 8

    def one_part(part, carry):
        start = pl.multiple_of(part * 8, 8)
        rows = pl.ds(start, 8)

        def one_k(k, inner):
            out_real = jnp.zeros((8, local), jnp.float32)
            out_imag = jnp.zeros((8, local), jnp.float32)
            for i in range(channels):
                real = jnp.broadcast_to(real_ref[k, i : i + 1, :], (8, local))
                imag = jnp.broadcast_to(imag_ref[k, i : i + 1, :], (8, local))
                w_real = w_ref[0, k, i, rows, :]
                w_imag = w_ref[1, k, i, rows, :]
                for alias in aliases[1:]:
                    w_real = w_real + w_ref[0, k + alias, i, rows, :]
                    w_imag = w_imag + w_ref[1, k + alias, i, rows, :]
                out_real = out_real + (real * w_real - imag * w_imag)
                out_imag = out_imag + (real * w_imag + imag * w_real)
            mixed[k] = jnp.concatenate([out_real, out_imag], axis=1)
            return inner

        lax.fori_loop(0, devices, one_k, 0)
        for x, value in enumerate(along_x([mixed[k] for k in range(devices)], -1)):
            src[pl.ds(x * channels + start, 8), :] = value

        @pl.when(part == 0)
        def _():
            meet_peers(devices)

        send_part(devices, channels, src, recv, sems, part)
        return carry

    lax.fori_loop(0, parts, one_part, 0)
    keep_own(channels, src, recv)

    def finish(part, carry):
        take_part(devices, channels, src, recv, sems, part)
        return carry

    lax.fori_loop(0, parts, finish, 0)
    for quad in range(channels // 4):
        rows = [
            recv[pl.ds(quad * 4 + c, devices, stride=channels), :] for c in range(4)
        ]
        for block in range(4):
            lanes = slice(block * MZ, (block + 1) * MZ)
            out_ref[
                block * devices : (block + 1) * devices, quad * 4 * MZ : (quad + 1) * 4 * MZ
            ] = jnp.concatenate([row[:, lanes] for row in rows], axis=1)


def mix_to_grid(real, imag, weights, devices):
    channels = real.shape[1]
    weights = pltpu.with_memory_space_constraint(weights.transpose(0, 1, 3, 4, 2), pltpu.VMEM)
    out = jax.ShapeDtypeStruct((4 * devices, channels * MZ), jnp.float32)
    vmem = pl.BlockSpec(memory_space=pltpu.VMEM)
    return pl.pallas_call(
        functools.partial(mix_kernel, devices, channels),
        out_shape=out,
        in_specs=[vmem, vmem, vmem],
        out_specs=vmem,
        scratch_shapes=[
            pltpu.VMEM((devices, 8, 4 * MZ), jnp.float32),
            pltpu.VMEM((devices * channels, 4 * MZ), jnp.float32),
            pltpu.VMEM((devices * channels, 4 * MZ), jnp.float32),
            pltpu.SemaphoreType.DMA((2, channels // 8, devices)),
        ],
        compiler_params=pltpu.CompilerParams(
            collective_id=1, has_side_effects=True, vmem_limit_bytes=8 * 2**20
        ),
        name="mix",
    )(real, imag, weights)


def x_table(length_x):
    return angles(np.arange(length_x), kept(MX, length_x), length_x)


def exchange_kernel(devices, src, out, send_sem, recv_sem, own_sem):
    me = lax.axis_index("space")
    barrier = pltpu.get_barrier_semaphore()

    def greet(step, carry):
        peer = lax.rem(me + step, devices)
        pl.semaphore_signal(
            barrier, inc=1, device_id={"space": peer}, device_id_type=pl.DeviceIdType.MESH
        )
        return carry

    def copy(step, slot):
        peer = lax.rem(me + step, devices)
        return pltpu.make_async_remote_copy(
            src_ref=src.at[peer],
            dst_ref=out.at[slot],
            send_sem=send_sem.at[step],
            recv_sem=recv_sem.at[step],
            device_id={"space": peer},
            device_id_type=pl.DeviceIdType.MESH,
        )

    def send(step, carry):
        copy(step, me).start()
        return carry

    def finish(step, carry):
        done = copy(step, lax.rem(me + devices - step, devices))
        done.wait_send()
        done.wait_recv()
        return carry

    lax.fori_loop(1, devices, greet, 0)
    own = pltpu.make_async_copy(src.at[me], out.at[me], own_sem)
    own.start()
    pl.semaphore_wait(barrier, devices - 1)
    lax.fori_loop(1, devices, send, 0)
    own.wait()
    lax.fori_loop(1, devices, finish, 0)


def exchange(lines, identity):
    devices = lax.axis_size("space")
    shape = lines.shape
    lines = lines.reshape(devices, -1, 128)
    vmem = pl.BlockSpec(memory_space=pltpu.VMEM)
    out = pl.pallas_call(
        functools.partial(exchange_kernel, devices),
        out_shape=jax.ShapeDtypeStruct(lines.shape, jnp.float32),
        in_specs=[vmem],
        out_specs=vmem,
        scratch_shapes=[
            pltpu.SemaphoreType.DMA((devices,)),
            pltpu.SemaphoreType.DMA((devices,)),
            pltpu.SemaphoreType.DMA,
        ],
        compiler_params=pltpu.CompilerParams(collective_id=identity, has_side_effects=True),
        name=f"exchange_{identity}",
    )(lines)
    return out.reshape(shape)


def to_spectrum(modes, scale, devices, extra=None):
    width, channels = modes.shape[:2]
    local = MY * MZ // devices
    lines = modes.reshape(width, channels, MY, 2, MZ).transpose(0, 3, 1, 2, 4)
    lines = lines.reshape(width, 2, channels, devices, local).transpose(3, 0, 1, 2, 4)
    lines = lines.reshape(devices, width * 2 * channels * local)
    size = lines.shape[1]
    if extra is not None:
        extra = jnp.pad(extra, (0, -extra.shape[0] % 128))
        extra = jnp.broadcast_to(extra[None], (devices,) + extra.shape)
        lines = jnp.concatenate([lines, extra], axis=1)
    lines = exchange(lines, 0 if extra is None else 2)
    summed = jnp.sum(lines[:, size:], axis=0)
    lines = lines[:, :size].reshape(devices * width, 2, channels, local)
    cos_x, sin_x = x_table(devices * width)
    table = np.stack([np.stack([cos_x, -sin_x], 1), np.stack([sin_x, cos_x], 1)], 1)
    table = jnp.asarray((table * scale).astype(np.float32))
    return jnp.einsum("xrcm,xrqk->qkcm", lines, table, precision=HIGH), summed


def mix_modes(spectrum, weights):
    real, imag = spectrum[0], spectrum[1]
    out_real = jnp.einsum("kim,kmio->kom", real, weights[0], precision=HIGH) - jnp.einsum(
        "kim,kmio->kom", imag, weights[1], precision=HIGH
    )
    out_imag = jnp.einsum("kim,kmio->kom", real, weights[1], precision=HIGH) + jnp.einsum(
        "kim,kmio->kom", imag, weights[0], precision=HIGH
    )
    return jnp.stack([out_real, out_imag], axis=0)


def to_grid(mixed, length_x):
    channels = mixed.shape[2]
    cos_x, sin_x = x_table(length_x)
    table = np.stack([np.stack([cos_x, sin_x], 0), np.stack([-sin_x, cos_x], 0)], 0)
    table = jnp.asarray(table.astype(np.float32))
    lines = jnp.einsum("rkom,rqxk->xqom", mixed, table, precision=HIGH)
    local = mixed.shape[3]
    devices = MY * MZ // local
    width = length_x // devices
    if local % MZ == 0:
        local_rows = local // MZ
        lines = lines.reshape(length_x, 2, channels, local_rows, MZ).transpose(0, 1, 3, 2, 4)
        lines = exchange(lines.reshape(length_x, 2 * local_rows * channels * MZ), 1)
        grid = lines.reshape(devices, width, 2 * local_rows, channels * MZ).transpose(1, 0, 2, 3)
    else:
        local_rows = 1
        lines = exchange(lines.reshape(length_x, 2 * channels * local), 1)
        grid = lines.reshape(MY, MZ // local, width, 2, channels, local).transpose(2, 0, 3, 4, 1, 5)
    return grid.reshape(width, 2 * MY, channels * MZ), local_rows


def body(lifted_field, cotangent, spectral_weights, point_weights, point_bias):
    devices = lax.axis_size("space")
    channels, width, ny, nz = lifted_field.shape
    length_x = width * devices
    scale = 1.0 / float(length_x * ny * nz) ** 0.5
    packed = width == 1 and MY == 2 * devices and MX % devices == 0 and channels % 8 == 0
    if packed:
        real, imag = front(lifted_field, devices, scale)
        grid_modes = mix_to_grid(real, imag, spectral_weights, devices)[None]
        local_rows = None
        spectrum = jnp.stack([real, imag], axis=0)
    else:
        spectrum, _ = to_spectrum(forward_modes(lifted_field), scale, devices)
        grid_modes, local_rows = to_grid(mix_modes(spectrum, spectral_weights), length_x)
    activated, slope_modes, wide_point = middle(
        grid_modes, local_rows, lifted_field, cotangent, point_weights, point_bias, scale
    )
    local_point = jnp.sum(wide_point.reshape(width, channels, channels, ROWS), axis=(0, 3))
    local_bias = jnp.sum(slope_modes[:, :, 0, 0], axis=0)
    partial = jnp.concatenate([local_point.reshape(-1), local_bias])
    slope_spectrum, summed = to_spectrum(slope_modes, scale, devices, partial)
    area = channels * channels
    summed_point = summed[:area].reshape(channels, channels)
    summed_bias = summed[area : area + channels]
    local_modes = spectrum.shape[3]
    mode_ids = lax.axis_index("space") * local_modes + jnp.arange(local_modes, dtype=jnp.int32)
    weight_modes = jnp.where(mode_ids % MZ == 0, 1.0, 2.0).astype(jnp.float32)
    grad_spectral = weight_gradient(spectrum, slope_spectrum * weight_modes)
    return (activated, grad_spectral, summed_point * scale, summed_bias * scale)


def solution(mesh):
    placed = (
        P("groups", "space", None, None),
        P("groups", "space", None, None),
        P(None, None, "space", None, None),
        P(),
        P(),
    )
    return jax.shard_map(
        body,
        mesh=mesh,
        in_specs=placed,
        out_specs=(
            P("groups", "space", None, None),
            P("groups", None, "space", None, None),
            P("groups", None),
            P("groups"),
        ),
        check_vma=False,
    )
```

```python
import functools

import jax
import jax.numpy as jnp
import numpy as np
from jax import lax
from jax.experimental import pallas as pl
from jax.experimental.pallas import tpu as pltpu
from jax.sharding import PartitionSpec as P

MX = 32
MY = 32
MZ = 32
ROWS = 8
STEP = 32

HIGH = lax.Precision.HIGH
INV_SQRT_TWO = 0.7071067811865476
INV_SQRT_TWO_PI = 0.3989422804014327


def angles(positions, frequency, length):
    product = np.outer(np.asarray(positions), np.asarray(frequency)) % length
    phase = 2.0 * np.pi / length * product.astype(np.float64)
    return np.cos(phase), np.sin(phase)


def kept(count, length):
    index = np.arange(count)
    return np.where(index < count // 2, index, length - count + index)


def halves(table):
    table = np.asarray(table, np.float32)
    high = table.astype(jnp.bfloat16)
    low = (table - high.astype(np.float32)).astype(jnp.bfloat16)
    return jnp.asarray(high), jnp.asarray(low)


def split(value):
    high = value.astype(jnp.bfloat16)
    low = (value - high.astype(jnp.float32)).astype(jnp.bfloat16)
    return high, low


def dot3(a, b, dims=(((1,), (0,)), ((), ()))):
    one = functools.partial(
        lax.dot_general, dimension_numbers=dims, preferred_element_type=jnp.float32
    )
    return one(a[0], b[0]) + (one(a[0], b[1]) + one(a[1], b[0]))


def forward_tables(ny, nz):
    cos_z, sin_z = angles(np.arange(nz), np.arange(MZ), nz)
    table_z = np.concatenate([cos_z, -sin_z, -sin_z, -cos_z], axis=1)
    cos_y, sin_y = angles(np.arange(ny), kept(MY, ny), ny)
    table_y = np.concatenate([cos_y.T, sin_y.T], axis=0)
    return halves(table_z) + halves(table_y)


def inverse_tables(ny, nz, scale, local_rows):
    cos_z, sin_z = angles(np.arange(nz), np.arange(MZ), nz)
    weight = np.where(np.arange(MZ) == 0, 1.0, 2.0)[:, None] * scale
    real = np.kron(np.eye(4), cos_z.T * weight)
    imag = np.kron(np.eye(4), -sin_z.T * weight)
    cos_y, sin_y = angles(np.arange(ny), kept(MY, ny), ny)
    if local_rows is None:
        cos_y = np.concatenate([cos_y[:, 0::2], cos_y[:, 1::2]], axis=1)
        sin_y = np.concatenate([sin_y[:, 0::2], sin_y[:, 1::2]], axis=1)
        real_y = np.concatenate([cos_y, -sin_y], axis=1)
        imag_y = np.concatenate([sin_y, cos_y], axis=1)
    else:
        cos_y = cos_y.reshape(ny, MY // local_rows, local_rows)
        sin_y = sin_y.reshape(ny, MY // local_rows, local_rows)
        real_y = np.stack([cos_y, -sin_y], 2).reshape(ny, 2 * MY)
        imag_y = np.stack([sin_y, cos_y], 2).reshape(ny, 2 * MY)
    return halves(np.concatenate([real, imag], 0)) + halves(np.concatenate([real_y, imag_y], 0))


def finish_y(lines, ty, modes_ref):
    def one(c, carry):
        both = dot3(ty, split(lines[c]))
        turned = pltpu.roll(both[MY:], 2 * MZ, 1)
        modes_ref[c] = (both[:MY] + turned)[:, : 2 * MZ]
        return carry

    lax.fori_loop(0, lines.shape[0], one, 0, unroll=16)


def forward_kernel(x_ref, tzh, tzl, tyh, tyl, modes_ref, lines):
    step = pl.program_id(1)
    channels, rows, nz = x_ref.shape
    value = x_ref[...].reshape(channels * rows, nz)
    along = dot3(split(value), (tzh[...], tzl[...]))
    start = pl.multiple_of(step * rows, rows)
    lines[:, pl.ds(start, rows), :] = along.reshape(channels, rows, 4 * MZ)

    @pl.when(step == pl.num_programs(1) - 1)
    def _():
        finish_y(lines, (tyh[...], tyl[...]), modes_ref)


def whole(array):
    shape = array.shape
    return pl.BlockSpec(shape, lambda *_: (0,) * len(shape))


def field_spec(channels, nz):
    return pl.BlockSpec((channels, None, STEP, nz), lambda x, y: (0, x, y, 0))


def modes_spec(channels):
    return pl.BlockSpec((None, channels, MY, 2 * MZ), lambda x, y: (x, 0, 0, 0))


def forward_modes(field):
    channels, width, ny, nz = field.shape
    tables = forward_tables(ny, nz)
    return pl.pallas_call(
        forward_kernel,
        grid=(width, ny // STEP),
        out_shape=jax.ShapeDtypeStruct((width, channels, MY, 2 * MZ), jnp.float32),
        in_specs=[field_spec(channels, nz)] + [whole(t) for t in tables],
        out_specs=modes_spec(channels),
        scratch_shapes=[pltpu.VMEM((channels, ny, 4 * MZ), jnp.float32)],
        name="forward_modes",
    )(field, *tables)


def middle_kernel(
    m_ref, x_ref, cot_ref, w_ref, bias_ref, pick, bdh, bdl, iyh, iyl, tzh, tzl, tyh, tyl,
    act_ref, modes_ref, point_ref, lines, inverse, field_part, wh, wl, total,
):
    step = pl.program_id(1)
    channels, rows, nz = x_ref.shape
    quads = channels // 4
    width = 4 * MZ
    ny = lines.shape[1]

    def same_row():
        size = channels * ROWS
        row = lax.broadcasted_iota(jnp.int32, (size, size), 0) % ROWS
        column = lax.broadcasted_iota(jnp.int32, (size, size), 1) % ROWS
        return row == column

    @pl.when(step == 0)
    def _():
        for part in range(0, m_ref.shape[1], 256):
            lanes = pl.ds(part, 256)
            both = dot3((iyh[...], iyl[...]), split(m_ref[:, lanes]))
            inverse[0, :, lanes] = both[:ny]
            inverse[1, :, lanes] = both[ny:]
        contract = (((1,), (1,)), ((), ()))
        for narrow, out in zip(split(w_ref[...]), (wh, wl)):
            tall = lax.dot_general(
                pick[...], narrow, contract, preferred_element_type=jnp.float32
            ).astype(jnp.bfloat16)
            square = lax.dot_general(tall, pick[...], contract, preferred_element_type=jnp.float32)
            out[...] = jnp.where(same_row(), square, 0.0).astype(jnp.bfloat16)
        total[...] = jnp.zeros_like(total)

    first = pl.multiple_of(step * rows, rows)
    stacked = jnp.concatenate(
        [
            jnp.concatenate(
                [
                    inverse[r, pl.ds(first, rows), g * width : (g + 1) * width]
                    for r in range(2)
                ],
                axis=1,
            )
            for g in range(quads)
        ],
        axis=0,
    )
    stacked = split(stacked)
    for c in range(4):
        lanes = slice(c * nz, (c + 1) * nz)
        field_part[:, lanes] = dot3(stacked, (bdh[:, lanes], bdl[:, lanes]))

    for half in range(rows // ROWS):
        here = slice(half * ROWS, (half + 1) * ROWS)
        start = pl.multiple_of(step * rows + half * ROWS, ROWS)
        spectral = jnp.concatenate(
            [
                field_part[
                    g * rows + half * ROWS : g * rows + (half + 1) * ROWS, c * nz : (c + 1) * nz
                ]
                for g in range(quads)
                for c in range(4)
            ],
            axis=0,
        )
        field = split(x_ref[:, here, :].reshape(channels * ROWS, nz))
        before = spectral + dot3((wh[...], wl[...]), field)
        before = before.reshape(channels, ROWS, nz) + bias_ref[...]
        normal = 0.5 * (1.0 + lax.erf(before * INV_SQRT_TWO))
        density = jnp.exp(-0.5 * before * before) * INV_SQRT_TWO_PI
        act_ref[:, here, :] = (before * normal).astype(jnp.bfloat16)
        slope = cot_ref[:, here, :].astype(jnp.float32) * (normal + before * density)
        slope = split(slope.reshape(channels * ROWS, nz))
        total[...] += dot3(field, slope, (((1,), (1,)), ((), ())))
        along = dot3(slope, (tzh[...], tzl[...]))
        lines[:, pl.ds(start, ROWS), :] = along.reshape(channels, ROWS, 4 * MZ)

    @pl.when(step == pl.num_programs(1) - 1)
    def _():
        finish_y(lines, (tyh[...], tyl[...]), modes_ref)
        size = channels * ROWS
        diagonal = jnp.where(same_row(), total[...], 0.0)
        point_ref[...] = jnp.sum(diagonal.reshape(channels, ROWS, size), axis=1)


def middle(grid_modes, local_rows, field, cotangent, point_weights, point_bias, scale):
    channels, width, ny, nz = field.shape
    size = channels * ROWS
    tables = inverse_tables(ny, nz, scale, local_rows) + forward_tables(ny, nz)
    pick = jnp.asarray(np.repeat(np.eye(channels, dtype=np.float32), ROWS, 0).astype(jnp.bfloat16))
    bias = jnp.broadcast_to(point_bias[:, None, None], (channels, 1, nz))
    spec = field_spec(channels, nz)
    mixed_spec = pl.BlockSpec((None,) + grid_modes.shape[1:], lambda x, y: (x, 0, 0))
    return pl.pallas_call(
        middle_kernel,
        grid=(width, ny // STEP),
        out_shape=(
            jax.ShapeDtypeStruct(field.shape, jnp.bfloat16),
            jax.ShapeDtypeStruct((width, channels, MY, 2 * MZ), jnp.float32),
            jax.ShapeDtypeStruct((width, channels, size), jnp.float32),
        ),
        in_specs=[mixed_spec, spec, spec, whole(point_weights), whole(bias), whole(pick)]
        + [whole(t) for t in tables],
        out_specs=(
            spec,
            modes_spec(channels),
            pl.BlockSpec((None, channels, size), lambda x, y: (x, 0, 0)),
        ),
        scratch_shapes=[
            pltpu.VMEM((channels, ny, 4 * MZ), jnp.float32),
            pltpu.VMEM((2, ny, channels * MZ), jnp.float32),
            pltpu.VMEM((channels // 4 * STEP, 4 * nz), jnp.float32),
            pltpu.VMEM((size, size), jnp.bfloat16),
            pltpu.VMEM((size, size), jnp.bfloat16),
            pltpu.VMEM((size, size), jnp.float32),
        ],
        name="middle",
    )(grid_modes, field, cotangent, point_weights, bias, pick, *tables)


def weight_gradient(spectrum, slope_modes):
    turned = jnp.stack([slope_modes[1], -slope_modes[0]], axis=0)
    slope_modes, turned = lax.optimization_barrier((slope_modes, turned))
    real = spectrum[0][None, :, :, None, :]
    imag = spectrum[1][None, :, :, None, :]
    out = real * slope_modes[:, :, None] + imag * turned[:, :, None]
    return out.transpose(0, 1, 4, 2, 3)


def packed_tables(ny, nz):
    cos_z, sin_z = angles(np.arange(nz), np.arange(MZ), nz)
    table_z = np.concatenate([cos_z, cos_z, -sin_z, -sin_z], axis=1)
    cos_y, sin_y = angles(np.arange(ny), kept(MY, ny), ny)
    cos_y, sin_y = cos_y.T, sin_y.T
    table_y = np.concatenate([cos_y[0::2], cos_y[1::2], sin_y[0::2], sin_y[1::2]], axis=0)
    return halves(table_z) + halves(table_y)


def lane_ids(rows):
    return lax.broadcasted_iota(jnp.int32, (rows, 4 * MZ), 1)


def turn(value):
    rolled = pltpu.roll(value, 2 * MZ, 1)
    return jnp.where(lane_ids(value.shape[0]) < 2 * MZ, rolled, -rolled)


def message_rows(ty, line):
    both = dot3(ty, split(line))
    count = MY // 2
    even = lane_ids(count) // MZ % 2 == 0
    cos_part = jnp.where(even, both[:count], both[count : 2 * count])
    sin_part = jnp.where(even, both[2 * count : 3 * count], both[3 * count :])
    return cos_part + turn(sin_part)


def along_x(parts, sign):
    length = len(parts)
    half = length // 2
    plus = [parts[x] + parts[length - x] for x in range(1, half)]
    minus = [turn(parts[x] - parts[length - x]) for x in range(1, half)]
    ends = (parts[0] + parts[half], parts[0] - parts[half])
    out = [None] * length
    for k in range(half + 1):
        even = ends[k % 2]
        odd = None
        for x in range(1, half):
            even = even + plus[x - 1] * float(np.cos(2 * np.pi * (k * x % length) / length))
            if 0 < k < half:
                term = minus[x - 1] * float(np.sin(2 * np.pi * (k * x % length) / length))
                odd = term if odd is None else odd + term
        if odd is None:
            out[k] = even
        else:
            out[k] = even + odd if sign > 0 else even - odd
            out[length - k] = even - odd if sign > 0 else even + odd
    return out


def greet_peers(devices):
    me = lax.axis_index("space")
    barrier = pltpu.get_barrier_semaphore()

    def greet(step, carry):
        pl.semaphore_signal(
            barrier,
            inc=1,
            device_id={"space": lax.rem(me + step, devices)},
            device_id_type=pl.DeviceIdType.MESH,
        )
        return carry

    lax.fori_loop(1, devices, greet, 0)


def meet_peers(devices):
    pl.semaphore_wait(pltpu.get_barrier_semaphore(), devices - 1)


def message(devices, channels, src, recv, sems, step, part, owner):
    me = lax.axis_index("space")
    peer = lax.rem(me + step, devices)
    there = pl.ds(pl.multiple_of(peer * channels + part * 8, 8), 8)
    here = pl.ds(pl.multiple_of(owner * channels + part * 8, 8), 8)
    return pltpu.make_async_remote_copy(
        src_ref=src.at[there],
        dst_ref=recv.at[here],
        send_sem=sems.at[0, part, step],
        recv_sem=sems.at[1, part, step],
        device_id={"space": peer},
        device_id_type=pl.DeviceIdType.MESH,
    )


def send_part(devices, channels, src, recv, sems, part):
    me = lax.axis_index("space")

    def send(step, carry):
        message(devices, channels, src, recv, sems, step, part, me).start()
        return carry

    lax.fori_loop(1, devices, send, 0)


def keep_own(channels, src, recv):
    me = lax.axis_index("space")
    own = pl.ds(pl.multiple_of(me * channels, channels), channels)
    recv[own, :] = src[own, :]


def take_part(devices, channels, src, recv, sems, part):
    me = lax.axis_index("space")

    def take(step, carry):
        owner = lax.rem(me + devices - step, devices)
        done = message(devices, channels, src, recv, sems, step, part, owner)
        done.wait_send()
        done.wait_recv()
        return carry

    lax.fori_loop(1, devices, take, 0)


def x_modes(devices, channels, scale, recv, part, real_ref, imag_ref):
    start = pl.multiple_of(part * 8, 8)
    parts = [recv[pl.ds(x * channels + start, 8), :] for x in range(devices)]
    for k, value in enumerate(along_x(parts, 1)):
        value = value * scale
        real, imag = value[:, : 2 * MZ], value[:, 2 * MZ :]
        for alias in range(k, real_ref.shape[0], devices):
            real_ref[alias, pl.ds(start, 8), :] = real
            imag_ref[alias, pl.ds(start, 8), :] = imag


def front_kernel(
    devices, channels, scale, x_ref, tzh, tzl, tyh, tyl, real_ref, imag_ref, lines, src, recv, sems
):
    part = pl.program_id(0)

    @pl.when(part == 0)
    def _():
        greet_peers(devices)

    rows, ny, nz = x_ref.shape
    value = x_ref[...].reshape(rows * ny, nz)
    along = dot3(split(value), (tzh[...], tzl[...]))
    lines[...] = along.reshape(rows, ny, 4 * MZ)
    ty = (tyh[...], tyl[...])
    for c in range(rows):
        src[pl.ds(part * rows + c, devices, stride=channels), :] = message_rows(ty, lines[c])

    @pl.when(part == 0)
    def _():
        meet_peers(devices)

    send_part(devices, channels, src, recv, sems, part)

    @pl.when(part == pl.num_programs(0) - 1)
    def _():
        keep_own(channels, src, recv)

        def finish(part, carry):
            take_part(devices, channels, src, recv, sems, part)
            x_modes(devices, channels, scale, recv, part, real_ref, imag_ref)
            return carry

        lax.fori_loop(0, channels // 8, finish, 0)


def front(field, devices, scale):
    channels, _, ny, nz = field.shape
    tables = packed_tables(ny, nz)
    parts = channels // 8
    spectrum = jax.ShapeDtypeStruct((MX, channels, 2 * MZ), jnp.float32)
    return pl.pallas_call(
        functools.partial(front_kernel, devices, channels, scale),
        grid=(parts,),
        out_shape=(spectrum, spectrum),
        in_specs=[pl.BlockSpec((8, None, ny, nz), lambda c: (c, 0, 0, 0))]
        + [whole(t) for t in tables],
        out_specs=(whole(spectrum), whole(spectrum)),
        scratch_shapes=[
            pltpu.VMEM((8, ny, 4 * MZ), jnp.float32),
            pltpu.VMEM((devices * channels, 4 * MZ), jnp.float32),
            pltpu.VMEM((devices * channels, 4 * MZ), jnp.float32),
            pltpu.SemaphoreType.DMA((2, parts, devices)),
        ],
        compiler_params=pltpu.CompilerParams(
            collective_id=0, has_side_effects=True
        ),
        name="front",
    )(field, *tables)


def mix_kernel(devices, channels, real_ref, imag_ref, w_ref, out_ref, mixed, src, recv, sems):
    greet_peers(devices)
    local = real_ref.shape[2]
    aliases = range(0, real_ref.shape[0], devices)
    parts = channels // 8

    def one_k(k, carry):
        totals = [jnp.zeros((8, local), jnp.float32)] * (2 * parts)
        for i in range(channels):
            real = jnp.broadcast_to(real_ref[k, i : i + 1, :], (8, local))
            imag = jnp.broadcast_to(imag_ref[k, i : i + 1, :], (8, local))
            for part in range(parts):
                rows = slice(part * 8, part * 8 + 8)
                w_real = w_ref[0, k, i, rows, :]
                w_imag = w_ref[1, k, i, rows, :]
                for alias in aliases[1:]:
                    w_real = w_real + w_ref[0, k + alias, i, rows, :]
                    w_imag = w_imag + w_ref[1, k + alias, i, rows, :]
                totals[2 * part] = totals[2 * part] + (real * w_real - imag * w_imag)
                totals[2 * part + 1] = totals[2 * part + 1] + (real * w_imag + imag * w_real)
        for part in range(parts):
            mixed[k, part] = jnp.concatenate(totals[2 * part : 2 * part + 2], axis=1)
        return carry

    lax.fori_loop(0, devices, one_k, 0)
    meet_peers(devices)

    def one_part(part, carry):
        start = pl.multiple_of(part * 8, 8)
        for x, value in enumerate(along_x([mixed[k, part] for k in range(devices)], -1)):
            src[pl.ds(x * channels + start, 8), :] = value
        send_part(devices, channels, src, recv, sems, part)
        return carry

    lax.fori_loop(0, parts, one_part, 0)
    keep_own(channels, src, recv)

    def finish(part, carry):
        take_part(devices, channels, src, recv, sems, part)
        return carry

    lax.fori_loop(0, parts, finish, 0)
    for quad in range(channels // 4):
        rows = [
            recv[pl.ds(quad * 4 + c, devices, stride=channels), :] for c in range(4)
        ]
        for block in range(4):
            lanes = slice(block * MZ, (block + 1) * MZ)
            out_ref[
                block * devices : (block + 1) * devices, quad * 4 * MZ : (quad + 1) * 4 * MZ
            ] = jnp.concatenate([row[:, lanes] for row in rows], axis=1)


def mix_to_grid(real, imag, weights, devices):
    channels = real.shape[1]
    weights = pltpu.with_memory_space_constraint(weights.transpose(0, 1, 3, 4, 2), pltpu.VMEM)
    out = jax.ShapeDtypeStruct((4 * devices, channels * MZ), jnp.float32)
    vmem = pl.BlockSpec(memory_space=pltpu.VMEM)
    return pl.pallas_call(
        functools.partial(mix_kernel, devices, channels),
        out_shape=out,
        in_specs=[vmem, vmem, vmem],
        out_specs=vmem,
        scratch_shapes=[
            pltpu.VMEM((devices, channels // 8, 8, 4 * MZ), jnp.float32),
            pltpu.VMEM((devices * channels, 4 * MZ), jnp.float32),
            pltpu.VMEM((devices * channels, 4 * MZ), jnp.float32),
            pltpu.SemaphoreType.DMA((2, channels // 8, devices)),
        ],
        compiler_params=pltpu.CompilerParams(
            collective_id=1, has_side_effects=True, vmem_limit_bytes=8 * 2**20
        ),
        name="mix",
    )(real, imag, weights)


def middle_packed_kernel(
    devices, m_ref, x_ref, cot_ref, w_ref, bias_ref, pick, bdh, bdl, iyh, iyl, tzh, tzl, tyh, tyl,
    act_ref, modes_ref, point_ref, lines, inverse, field_part, wh, wl, total, bias, point,
):
    step = pl.program_id(1)
    channels, rows, nz = x_ref.shape
    quads = channels // 4
    width = 4 * MZ
    ny = lines.shape[1]

    def same_row():
        size = channels * ROWS
        row = lax.broadcasted_iota(jnp.int32, (size, size), 0) % ROWS
        column = lax.broadcasted_iota(jnp.int32, (size, size), 1) % ROWS
        return row == column

    @pl.when(step == 0)
    def _():
        for part in range(0, m_ref.shape[1], 256):
            lanes = pl.ds(part, 256)
            both = dot3((iyh[...], iyl[...]), split(m_ref[:, lanes]))
            inverse[0, :, lanes] = both[:ny]
            inverse[1, :, lanes] = both[ny:]
        contract = (((1,), (1,)), ((), ()))
        for narrow, out in zip(split(w_ref[...]), (wh, wl)):
            tall = lax.dot_general(
                pick[...], narrow, contract, preferred_element_type=jnp.float32
            ).astype(jnp.bfloat16)
            square = lax.dot_general(tall, pick[...], contract, preferred_element_type=jnp.float32)
            out[...] = jnp.where(same_row(), square, 0.0).astype(jnp.bfloat16)
        total[...] = jnp.zeros_like(total)
        rest = jnp.broadcast_to(bias_ref[...], (nz, channels))
        wide = jnp.zeros_like(bias)
        for _ in range(3):
            narrow = rest.astype(jnp.bfloat16)
            rest = rest - narrow.astype(jnp.float32)
            wide = wide + lax.dot_general(
                pick[...], narrow, contract, preferred_element_type=jnp.float32
            )
        bias[...] = wide

    first = pl.multiple_of(step * rows, rows)
    stacked = jnp.concatenate(
        [
            jnp.concatenate(
                [
                    inverse[r, pl.ds(first, rows), g * width : (g + 1) * width]
                    for r in range(2)
                ],
                axis=1,
            )
            for g in range(quads)
        ],
        axis=0,
    )
    stacked = split(stacked)
    for c in range(4):
        lanes = slice(c * nz, (c + 1) * nz)
        field_part[:, lanes] = dot3(stacked, (bdh[:, lanes], bdl[:, lanes]))

    for half in range(rows // ROWS):
        here = slice(half * ROWS, (half + 1) * ROWS)
        start = pl.multiple_of(step * rows + half * ROWS, ROWS)
        spectral = jnp.concatenate(
            [
                field_part[
                    g * rows + half * ROWS : g * rows + (half + 1) * ROWS, c * nz : (c + 1) * nz
                ]
                for g in range(quads)
                for c in range(4)
            ],
            axis=0,
        )
        field = split(x_ref[:, here, :].reshape(channels * ROWS, nz))
        before = spectral + dot3((wh[...], wl[...]), field)
        before = (before + bias[...]).reshape(channels, ROWS, nz)
        normal = 0.5 * (1.0 + lax.erf(before * INV_SQRT_TWO))
        density = jnp.exp(-0.5 * before * before) * INV_SQRT_TWO_PI
        act_ref[:, here, :] = (before * normal).astype(jnp.bfloat16)
        slope = cot_ref[:, here, :].astype(jnp.float32) * (normal + before * density)
        slope = split(slope.reshape(channels * ROWS, nz))
        total[...] += dot3(field, slope, (((1,), (1,)), ((), ())))
        along = dot3(slope, (tzh[...], tzl[...]))
        lines[:, pl.ds(start, ROWS), :] = along.reshape(channels, ROWS, 4 * MZ)

    @pl.when(step == pl.num_programs(1) - 1)
    def _():
        ty = (tyh[...], tyl[...])

        def finish(c, carry):
            modes_ref[pl.ds(c, devices, stride=channels), :] = message_rows(ty, lines[c])
            return carry

        lax.fori_loop(0, channels, finish, 0, unroll=8)
        diagonal = jnp.where(same_row(), total[...], 0.0)
        rows_sum = jnp.sum(diagonal.reshape(channels, ROWS, channels * ROWS), axis=1)
        high, low = split(rows_sum)
        folded = jnp.dot(high, pick[...], preferred_element_type=jnp.float32) + jnp.dot(
            low, pick[...], preferred_element_type=jnp.float32
        )
        own_bias = modes_ref[:channels, :channels]
        lane = lax.broadcasted_iota(jnp.int32, (channels, channels), 1)
        own_bias = jnp.where(lane == 0, own_bias, 0.0)
        spare = jnp.zeros((channels, 4 * MZ - 2 * channels), jnp.float32)
        point[...] = jnp.concatenate([folded, own_bias, spare], axis=1)
        first_rows = point[pl.ds(0, channels // 2, stride=2), :]
        second_rows = point[pl.ds(1, channels // 2, stride=2), :]
        packed = first_rows + pltpu.roll(second_rows, 2 * MZ, 1)
        for d in range(channels // 2):
            point_ref[d] = packed[d : d + 1]


def middle_packed(grid_modes, devices, field, cotangent, point_weights, point_bias, scale):
    channels, width, ny, nz = field.shape
    size = channels * ROWS
    tables = inverse_tables(ny, nz, scale, None) + packed_tables(ny, nz)
    pick = jnp.asarray(np.repeat(np.eye(channels, dtype=np.float32), ROWS, 0).astype(jnp.bfloat16))
    bias = point_bias.reshape(1, channels)
    spec = field_spec(channels, nz)
    mixed_spec = pl.BlockSpec((None,) + grid_modes.shape[1:], lambda x, y: (x, 0, 0))
    return pl.pallas_call(
        functools.partial(middle_packed_kernel, devices),
        grid=(width, ny // STEP),
        out_shape=(
            jax.ShapeDtypeStruct(field.shape, jnp.bfloat16),
            jax.ShapeDtypeStruct((devices * channels, 4 * MZ), jnp.float32),
            jax.ShapeDtypeStruct((channels // 2, 1, 4 * MZ), jnp.float32),
        ),
        in_specs=[mixed_spec, spec, spec, whole(point_weights), whole(bias), whole(pick)]
        + [whole(t) for t in tables],
        out_specs=(
            spec,
            pl.BlockSpec((devices * channels, 4 * MZ), lambda x, y: (0, 0)),
            pl.BlockSpec((channels // 2, 1, 4 * MZ), lambda x, y: (0, 0, 0)),
        ),
        scratch_shapes=[
            pltpu.VMEM((channels, ny, 4 * MZ), jnp.float32),
            pltpu.VMEM((2, ny, channels * MZ), jnp.float32),
            pltpu.VMEM((channels // 4 * STEP, 4 * nz), jnp.float32),
            pltpu.VMEM((size, size), jnp.bfloat16),
            pltpu.VMEM((size, size), jnp.bfloat16),
            pltpu.VMEM((size, size), jnp.float32),
            pltpu.VMEM((size, nz), jnp.float32),
            pltpu.VMEM((channels, 4 * MZ), jnp.float32),
        ],
        name="middle_packed",
    )(grid_modes, field, cotangent, point_weights, bias, pick, *tables)


def tail_kernel(
    devices, channels, scale, src, point_ref, slope_ref, turned_ref, sums_ref, bias_ref,
    recv, partial, total, gathered, sems, point_sems,
):
    me = lax.axis_index("space")
    greet_peers(devices)
    meet_peers(devices)

    def point_message(step, phase, source, target):
        peer = lax.rem(me + step, devices)
        return pltpu.make_async_remote_copy(
            src_ref=source(peer),
            dst_ref=target,
            send_sem=point_sems.at[phase, 0, step],
            recv_sem=point_sems.at[phase, 1, step],
            device_id={"space": peer},
            device_id_type=pl.DeviceIdType.MESH,
        )

    def scatter(step, owner):
        return point_message(step, 0, lambda peer: point_ref.at[peer], partial.at[owner])

    def gather(step, owner):
        return point_message(step, 1, lambda peer: total, gathered.at[owner])

    def start(make):
        def one(step, carry):
            make(step, me).start()
            return carry

        lax.fori_loop(1, devices, one, 0)

    def finish(make):
        def one(step, carry):
            done = make(step, lax.rem(me + devices - step, devices))
            done.wait_send()
            done.wait_recv()
            return carry

        lax.fori_loop(1, devices, one, 0)

    start(scatter)
    for part in range(channels // 8):
        send_part(devices, channels, src, recv, sems, part)
    keep_own(channels, src, recv)
    partial[me] = point_ref[me]
    finish(scatter)
    summed = partial[0]
    for d in range(1, devices):
        summed = summed + partial[d]
    total[...] = summed * scale
    start(gather)
    gathered[me] = total[...]
    weight = jnp.where(lane_ids(8) % MZ == 0, scale, 2.0 * scale)

    def one_part(part, carry):
        take_part(devices, channels, src, recv, sems, part)
        first = pl.multiple_of(part * 8, 8)
        rows = pl.ds(first, 8)
        parts = [recv[pl.ds(x * channels + first, 8), :] for x in range(devices)]
        for k, value in enumerate(along_x(parts, 1)):
            value = value * weight
            real, imag = value[:, : 2 * MZ], value[:, 2 * MZ :]
            for alias in range(k, slope_ref.shape[1], devices):
                slope_ref[0, alias, rows, :] = real
                slope_ref[1, alias, rows, :] = imag
                turned_ref[0, alias, rows, :] = imag
                turned_ref[1, alias, rows, :] = -real
        return carry

    lax.fori_loop(0, channels // 8, one_part, 0)
    finish(gather)
    for d in range(devices):
        row = gathered[d]
        both = jnp.concatenate([row[:, : 2 * MZ], row[:, 2 * MZ :]], axis=0)
        sums_ref[2 * d : 2 * d + 2, :] = both[:, :channels]
        bias_ref[2 * d : 2 * d + 2, :] = both[:, channels : channels + 1]


def tail(modes, point, devices, scale):
    channels = modes.shape[0] // devices
    parts = channels // 8
    vmem = pl.BlockSpec(memory_space=pltpu.VMEM)
    slope = jax.ShapeDtypeStruct((2, MX, channels, 2 * MZ), jnp.float32)
    return pl.pallas_call(
        functools.partial(tail_kernel, devices, channels, scale),
        out_shape=(
            slope,
            slope,
            jax.ShapeDtypeStruct((channels, channels), jnp.float32),
            jax.ShapeDtypeStruct((channels, 1), jnp.float32),
        ),
        in_specs=[vmem] * 2,
        out_specs=(vmem,) * 4,
        scratch_shapes=[
            pltpu.VMEM((devices * channels, 4 * MZ), jnp.float32),
            pltpu.VMEM((devices, 1, 4 * MZ), jnp.float32),
            pltpu.VMEM((1, 4 * MZ), jnp.float32),
            pltpu.VMEM((devices, 1, 4 * MZ), jnp.float32),
            pltpu.SemaphoreType.DMA((2, parts, devices)),
            pltpu.SemaphoreType.DMA((2, 2, devices)),
        ],
        compiler_params=pltpu.CompilerParams(collective_id=2, has_side_effects=True, vmem_limit_bytes=8 * 2**20),
        name="tail",
    )(modes, point)


def x_table(length_x):
    return angles(np.arange(length_x), kept(MX, length_x), length_x)


def exchange_kernel(devices, src, out, send_sem, recv_sem, own_sem):
    me = lax.axis_index("space")
    barrier = pltpu.get_barrier_semaphore()

    def greet(step, carry):
        peer = lax.rem(me + step, devices)
        pl.semaphore_signal(
            barrier, inc=1, device_id={"space": peer}, device_id_type=pl.DeviceIdType.MESH
        )
        return carry

    def copy(step, slot):
        peer = lax.rem(me + step, devices)
        return pltpu.make_async_remote_copy(
            src_ref=src.at[peer],
            dst_ref=out.at[slot],
            send_sem=send_sem.at[step],
            recv_sem=recv_sem.at[step],
            device_id={"space": peer},
            device_id_type=pl.DeviceIdType.MESH,
        )

    def send(step, carry):
        copy(step, me).start()
        return carry

    def finish(step, carry):
        done = copy(step, lax.rem(me + devices - step, devices))
        done.wait_send()
        done.wait_recv()
        return carry

    lax.fori_loop(1, devices, greet, 0)
    own = pltpu.make_async_copy(src.at[me], out.at[me], own_sem)
    own.start()
    pl.semaphore_wait(barrier, devices - 1)
    lax.fori_loop(1, devices, send, 0)
    own.wait()
    lax.fori_loop(1, devices, finish, 0)


def exchange(lines, identity):
    devices = lax.axis_size("space")
    shape = lines.shape
    lines = lines.reshape(devices, -1, 128)
    vmem = pl.BlockSpec(memory_space=pltpu.VMEM)
    out = pl.pallas_call(
        functools.partial(exchange_kernel, devices),
        out_shape=jax.ShapeDtypeStruct(lines.shape, jnp.float32),
        in_specs=[vmem],
        out_specs=vmem,
        scratch_shapes=[
            pltpu.SemaphoreType.DMA((devices,)),
            pltpu.SemaphoreType.DMA((devices,)),
            pltpu.SemaphoreType.DMA,
        ],
        compiler_params=pltpu.CompilerParams(collective_id=identity, has_side_effects=True),
        name=f"exchange_{identity}",
    )(lines)
    return out.reshape(shape)


def to_spectrum(modes, scale, devices, extra=None):
    width, channels = modes.shape[:2]
    local = MY * MZ // devices
    lines = modes.reshape(width, channels, MY, 2, MZ).transpose(0, 3, 1, 2, 4)
    lines = lines.reshape(width, 2, channels, devices, local).transpose(3, 0, 1, 2, 4)
    lines = lines.reshape(devices, width * 2 * channels * local)
    size = lines.shape[1]
    if extra is not None:
        extra = jnp.pad(extra, (0, -extra.shape[0] % 128))
        extra = jnp.broadcast_to(extra[None], (devices,) + extra.shape)
        lines = jnp.concatenate([lines, extra], axis=1)
    lines = exchange(lines, 0 if extra is None else 2)
    summed = jnp.sum(lines[:, size:], axis=0)
    lines = lines[:, :size].reshape(devices * width, 2, channels, local)
    cos_x, sin_x = x_table(devices * width)
    table = np.stack([np.stack([cos_x, -sin_x], 1), np.stack([sin_x, cos_x], 1)], 1)
    table = jnp.asarray((table * scale).astype(np.float32))
    return jnp.einsum("xrcm,xrqk->qkcm", lines, table, precision=HIGH), summed


def mix_modes(spectrum, weights):
    real, imag = spectrum[0], spectrum[1]
    out_real = jnp.einsum("kim,kmio->kom", real, weights[0], precision=HIGH) - jnp.einsum(
        "kim,kmio->kom", imag, weights[1], precision=HIGH
    )
    out_imag = jnp.einsum("kim,kmio->kom", real, weights[1], precision=HIGH) + jnp.einsum(
        "kim,kmio->kom", imag, weights[0], precision=HIGH
    )
    return jnp.stack([out_real, out_imag], axis=0)


def to_grid(mixed, length_x):
    channels = mixed.shape[2]
    cos_x, sin_x = x_table(length_x)
    table = np.stack([np.stack([cos_x, sin_x], 0), np.stack([-sin_x, cos_x], 0)], 0)
    table = jnp.asarray(table.astype(np.float32))
    lines = jnp.einsum("rkom,rqxk->xqom", mixed, table, precision=HIGH)
    local = mixed.shape[3]
    devices = MY * MZ // local
    width = length_x // devices
    if local % MZ == 0:
        local_rows = local // MZ
        lines = lines.reshape(length_x, 2, channels, local_rows, MZ).transpose(0, 1, 3, 2, 4)
        lines = exchange(lines.reshape(length_x, 2 * local_rows * channels * MZ), 1)
        grid = lines.reshape(devices, width, 2 * local_rows, channels * MZ).transpose(1, 0, 2, 3)
    else:
        local_rows = 1
        lines = exchange(lines.reshape(length_x, 2 * channels * local), 1)
        grid = lines.reshape(MY, MZ // local, width, 2, channels, local).transpose(2, 0, 3, 4, 1, 5)
    return grid.reshape(width, 2 * MY, channels * MZ), local_rows


def body(lifted_field, cotangent, spectral_weights, point_weights, point_bias):
    devices = lax.axis_size("space")
    channels, width, ny, nz = lifted_field.shape
    length_x = width * devices
    scale = 1.0 / float(length_x * ny * nz) ** 0.5
    packed = width == 1 and MY == 2 * devices == channels and MX % devices == 0
    if packed:
        real, imag = front(lifted_field, devices, scale)
        grid_modes = mix_to_grid(real, imag, spectral_weights, devices)[None]
        activated, modes, point = middle_packed(
            grid_modes, devices, lifted_field, cotangent, point_weights, point_bias, scale
        )
        slope, turned, summed_point, summed_bias = tail(modes, point, devices, scale)
        grad_spectral = real[None, :, :, None] * slope[:, :, None] + imag[None, :, :, None] * turned[:, :, None]
        return (
            activated,
            grad_spectral.transpose(0, 1, 4, 2, 3),
            summed_point,
            summed_bias.reshape(-1),
        )
    else:
        spectrum, _ = to_spectrum(forward_modes(lifted_field), scale, devices)
        grid_modes, local_rows = to_grid(mix_modes(spectrum, spectral_weights), length_x)
    activated, slope_modes, wide_point = middle(
        grid_modes, local_rows, lifted_field, cotangent, point_weights, point_bias, scale
    )
    local_point = jnp.sum(wide_point.reshape(width, channels, channels, ROWS), axis=(0, 3))
    local_bias = jnp.sum(slope_modes[:, :, 0, 0], axis=0)
    partial = jnp.concatenate([local_point.reshape(-1), local_bias])
    slope_spectrum, summed = to_spectrum(slope_modes, scale, devices, partial)
    area = channels * channels
    summed_point = summed[:area].reshape(channels, channels)
    summed_bias = summed[area : area + channels]
    local_modes = spectrum.shape[3]
    mode_ids = lax.axis_index("space") * local_modes + jnp.arange(local_modes, dtype=jnp.int32)
    weight_modes = jnp.where(mode_ids % MZ == 0, 1.0, 2.0).astype(jnp.float32)
    grad_spectral = weight_gradient(spectrum, slope_spectrum * weight_modes)
    return (activated, grad_spectral, summed_point * scale, summed_bias * scale)


def solution(mesh):
    placed = (
        P("groups", "space", None, None),
        P("groups", "space", None, None),
        P(None, None, "space", None, None),
        P(),
        P(),
    )
    return jax.shard_map(
        body,
        mesh=mesh,
        in_specs=placed,
        out_specs=(
            P("groups", "space", None, None),
            P("groups", None, "space", None, None),
            P("groups", None),
            P("groups"),
        ),
        check_vma=False,
    )
```

```python
import functools

import jax
import jax.numpy as jnp
import numpy as np
from jax import lax
from jax.experimental import pallas as pl
from jax.experimental.pallas import tpu as pltpu
from jax.sharding import PartitionSpec as P

MX = 32
MY = 32
MZ = 32
ROWS = 8
STEP = 32

HIGH = lax.Precision.HIGH
INV_SQRT_TWO = 0.7071067811865476
INV_SQRT_TWO_PI = 0.3989422804014327


def angles(positions, frequency, length):
    product = np.outer(np.asarray(positions), np.asarray(frequency)) % length
    phase = 2.0 * np.pi / length * product.astype(np.float64)
    return np.cos(phase), np.sin(phase)


def kept(count, length):
    index = np.arange(count)
    return np.where(index < count // 2, index, length - count + index)


def halves(table):
    table = np.asarray(table, np.float32)
    high = table.astype(jnp.bfloat16)
    low = (table - high.astype(np.float32)).astype(jnp.bfloat16)
    return jnp.asarray(high), jnp.asarray(low)


def split(value):
    high = value.astype(jnp.bfloat16)
    low = (value - high.astype(jnp.float32)).astype(jnp.bfloat16)
    return high, low


def dot3(a, b, dims=(((1,), (0,)), ((), ()))):
    one = functools.partial(
        lax.dot_general, dimension_numbers=dims, preferred_element_type=jnp.float32
    )
    return one(a[0], b[0]) + (one(a[0], b[1]) + one(a[1], b[0]))


def forward_tables(ny, nz):
    cos_z, sin_z = angles(np.arange(nz), np.arange(MZ), nz)
    table_z = np.concatenate([cos_z, -sin_z, -sin_z, -cos_z], axis=1)
    cos_y, sin_y = angles(np.arange(ny), kept(MY, ny), ny)
    table_y = np.concatenate([cos_y.T, sin_y.T], axis=0)
    return halves(table_z) + halves(table_y)


def inverse_tables(ny, nz, scale, local_rows):
    cos_z, sin_z = angles(np.arange(nz), np.arange(MZ), nz)
    weight = np.where(np.arange(MZ) == 0, 1.0, 2.0)[:, None] * scale
    real = np.kron(np.eye(4), cos_z.T * weight)
    imag = np.kron(np.eye(4), -sin_z.T * weight)
    cos_y, sin_y = angles(np.arange(ny), kept(MY, ny), ny)
    if local_rows is None:
        cos_y = np.concatenate([cos_y[:, 0::2], cos_y[:, 1::2]], axis=1)
        sin_y = np.concatenate([sin_y[:, 0::2], sin_y[:, 1::2]], axis=1)
        real_y = np.concatenate([cos_y, -sin_y], axis=1)
        imag_y = np.concatenate([sin_y, cos_y], axis=1)
    else:
        cos_y = cos_y.reshape(ny, MY // local_rows, local_rows)
        sin_y = sin_y.reshape(ny, MY // local_rows, local_rows)
        real_y = np.stack([cos_y, -sin_y], 2).reshape(ny, 2 * MY)
        imag_y = np.stack([sin_y, cos_y], 2).reshape(ny, 2 * MY)
    return halves(np.concatenate([real, imag], 0)) + halves(np.concatenate([real_y, imag_y], 0))


def finish_y(lines, ty, modes_ref):
    def one(c, carry):
        both = dot3(ty, split(lines[c]))
        turned = pltpu.roll(both[MY:], 2 * MZ, 1)
        modes_ref[c] = (both[:MY] + turned)[:, : 2 * MZ]
        return carry

    lax.fori_loop(0, lines.shape[0], one, 0, unroll=16)


def forward_kernel(x_ref, tzh, tzl, tyh, tyl, modes_ref, lines):
    step = pl.program_id(1)
    channels, rows, nz = x_ref.shape
    value = x_ref[...].reshape(channels * rows, nz)
    along = dot3(split(value), (tzh[...], tzl[...]))
    start = pl.multiple_of(step * rows, rows)
    lines[:, pl.ds(start, rows), :] = along.reshape(channels, rows, 4 * MZ)

    @pl.when(step == pl.num_programs(1) - 1)
    def _():
        finish_y(lines, (tyh[...], tyl[...]), modes_ref)


def whole(array):
    shape = array.shape
    return pl.BlockSpec(shape, lambda *_: (0,) * len(shape))


def field_spec(channels, nz):
    return pl.BlockSpec((channels, None, STEP, nz), lambda x, y: (0, x, y, 0))


def modes_spec(channels):
    return pl.BlockSpec((None, channels, MY, 2 * MZ), lambda x, y: (x, 0, 0, 0))


def forward_modes(field):
    channels, width, ny, nz = field.shape
    tables = forward_tables(ny, nz)
    return pl.pallas_call(
        forward_kernel,
        grid=(width, ny // STEP),
        out_shape=jax.ShapeDtypeStruct((width, channels, MY, 2 * MZ), jnp.float32),
        in_specs=[field_spec(channels, nz)] + [whole(t) for t in tables],
        out_specs=modes_spec(channels),
        scratch_shapes=[pltpu.VMEM((channels, ny, 4 * MZ), jnp.float32)],
        name="forward_modes",
    )(field, *tables)


def middle_kernel(
    m_ref, x_ref, cot_ref, w_ref, bias_ref, pick, bdh, bdl, iyh, iyl, tzh, tzl, tyh, tyl,
    act_ref, modes_ref, point_ref, lines, inverse, field_part, wh, wl, total,
):
    step = pl.program_id(1)
    channels, rows, nz = x_ref.shape
    quads = channels // 4
    width = 4 * MZ
    ny = lines.shape[1]

    def same_row():
        size = channels * ROWS
        row = lax.broadcasted_iota(jnp.int32, (size, size), 0) % ROWS
        column = lax.broadcasted_iota(jnp.int32, (size, size), 1) % ROWS
        return row == column

    @pl.when(step == 0)
    def _():
        for part in range(0, m_ref.shape[1], 256):
            lanes = pl.ds(part, 256)
            both = dot3((iyh[...], iyl[...]), split(m_ref[:, lanes]))
            inverse[0, :, lanes] = both[:ny]
            inverse[1, :, lanes] = both[ny:]
        contract = (((1,), (1,)), ((), ()))
        for narrow, out in zip(split(w_ref[...]), (wh, wl)):
            tall = lax.dot_general(
                pick[...], narrow, contract, preferred_element_type=jnp.float32
            ).astype(jnp.bfloat16)
            square = lax.dot_general(tall, pick[...], contract, preferred_element_type=jnp.float32)
            out[...] = jnp.where(same_row(), square, 0.0).astype(jnp.bfloat16)
        total[...] = jnp.zeros_like(total)

    first = pl.multiple_of(step * rows, rows)
    stacked = jnp.concatenate(
        [
            jnp.concatenate(
                [
                    inverse[r, pl.ds(first, rows), g * width : (g + 1) * width]
                    for r in range(2)
                ],
                axis=1,
            )
            for g in range(quads)
        ],
        axis=0,
    )
    stacked = split(stacked)
    for c in range(4):
        lanes = slice(c * nz, (c + 1) * nz)
        field_part[:, lanes] = dot3(stacked, (bdh[:, lanes], bdl[:, lanes]))

    for half in range(rows // ROWS):
        here = slice(half * ROWS, (half + 1) * ROWS)
        start = pl.multiple_of(step * rows + half * ROWS, ROWS)
        spectral = jnp.concatenate(
            [
                field_part[
                    g * rows + half * ROWS : g * rows + (half + 1) * ROWS, c * nz : (c + 1) * nz
                ]
                for g in range(quads)
                for c in range(4)
            ],
            axis=0,
        )
        field = split(x_ref[:, here, :].reshape(channels * ROWS, nz))
        before = spectral + dot3((wh[...], wl[...]), field)
        before = before.reshape(channels, ROWS, nz) + bias_ref[...]
        normal = 0.5 * (1.0 + lax.erf(before * INV_SQRT_TWO))
        density = jnp.exp(-0.5 * before * before) * INV_SQRT_TWO_PI
        act_ref[:, here, :] = (before * normal).astype(jnp.bfloat16)
        slope = cot_ref[:, here, :].astype(jnp.float32) * (normal + before * density)
        slope = split(slope.reshape(channels * ROWS, nz))
        total[...] += dot3(field, slope, (((1,), (1,)), ((), ())))
        along = dot3(slope, (tzh[...], tzl[...]))
        lines[:, pl.ds(start, ROWS), :] = along.reshape(channels, ROWS, 4 * MZ)

    @pl.when(step == pl.num_programs(1) - 1)
    def _():
        finish_y(lines, (tyh[...], tyl[...]), modes_ref)
        size = channels * ROWS
        diagonal = jnp.where(same_row(), total[...], 0.0)
        point_ref[...] = jnp.sum(diagonal.reshape(channels, ROWS, size), axis=1)


def middle(grid_modes, local_rows, field, cotangent, point_weights, point_bias, scale):
    channels, width, ny, nz = field.shape
    size = channels * ROWS
    tables = inverse_tables(ny, nz, scale, local_rows) + forward_tables(ny, nz)
    pick = jnp.asarray(np.repeat(np.eye(channels, dtype=np.float32), ROWS, 0).astype(jnp.bfloat16))
    bias = jnp.broadcast_to(point_bias[:, None, None], (channels, 1, nz))
    spec = field_spec(channels, nz)
    mixed_spec = pl.BlockSpec((None,) + grid_modes.shape[1:], lambda x, y: (x, 0, 0))
    return pl.pallas_call(
        middle_kernel,
        grid=(width, ny // STEP),
        out_shape=(
            jax.ShapeDtypeStruct(field.shape, jnp.bfloat16),
            jax.ShapeDtypeStruct((width, channels, MY, 2 * MZ), jnp.float32),
            jax.ShapeDtypeStruct((width, channels, size), jnp.float32),
        ),
        in_specs=[mixed_spec, spec, spec, whole(point_weights), whole(bias), whole(pick)]
        + [whole(t) for t in tables],
        out_specs=(
            spec,
            modes_spec(channels),
            pl.BlockSpec((None, channels, size), lambda x, y: (x, 0, 0)),
        ),
        scratch_shapes=[
            pltpu.VMEM((channels, ny, 4 * MZ), jnp.float32),
            pltpu.VMEM((2, ny, channels * MZ), jnp.float32),
            pltpu.VMEM((channels // 4 * STEP, 4 * nz), jnp.float32),
            pltpu.VMEM((size, size), jnp.bfloat16),
            pltpu.VMEM((size, size), jnp.bfloat16),
            pltpu.VMEM((size, size), jnp.float32),
        ],
        name="middle",
    )(grid_modes, field, cotangent, point_weights, bias, pick, *tables)


def weight_gradient(spectrum, slope_modes):
    turned = jnp.stack([slope_modes[1], -slope_modes[0]], axis=0)
    slope_modes, turned = lax.optimization_barrier((slope_modes, turned))
    real = spectrum[0][None, :, :, None, :]
    imag = spectrum[1][None, :, :, None, :]
    out = real * slope_modes[:, :, None] + imag * turned[:, :, None]
    return out.transpose(0, 1, 4, 2, 3)


def packed_tables(ny, nz):
    cos_z, sin_z = angles(np.arange(nz), np.arange(MZ), nz)
    table_z = np.concatenate([cos_z, cos_z, -sin_z, -sin_z], axis=1)
    cos_y, sin_y = angles(np.arange(ny), kept(MY, ny), ny)
    cos_y, sin_y = cos_y.T, sin_y.T
    table_y = np.concatenate([cos_y[0::2], cos_y[1::2], sin_y[0::2], sin_y[1::2]], axis=0)
    return halves(table_z) + halves(table_y)


def lane_ids(rows):
    return lax.broadcasted_iota(jnp.int32, (rows, 4 * MZ), 1)


def turn(value):
    rolled = pltpu.roll(value, 2 * MZ, 1)
    return jnp.where(lane_ids(value.shape[0]) < 2 * MZ, rolled, -rolled)


def message_rows(ty, line):
    both = dot3(ty, split(line))
    count = MY // 2
    even = lane_ids(count) // MZ % 2 == 0
    cos_part = jnp.where(even, both[:count], both[count : 2 * count])
    sin_part = jnp.where(even, both[2 * count : 3 * count], both[3 * count :])
    return cos_part + turn(sin_part)


def along_x(parts, sign):
    length = len(parts)
    half = length // 2
    plus = [parts[x] + parts[length - x] for x in range(1, half)]
    minus = [turn(parts[x] - parts[length - x]) for x in range(1, half)]
    ends = (parts[0] + parts[half], parts[0] - parts[half])
    out = [None] * length
    for k in range(half + 1):
        even = ends[k % 2]
        odd = None
        for x in range(1, half):
            even = even + plus[x - 1] * float(np.cos(2 * np.pi * (k * x % length) / length))
            if 0 < k < half:
                term = minus[x - 1] * float(np.sin(2 * np.pi * (k * x % length) / length))
                odd = term if odd is None else odd + term
        if odd is None:
            out[k] = even
        else:
            out[k] = even + odd if sign > 0 else even - odd
            out[length - k] = even - odd if sign > 0 else even + odd
    return out


def greet_peers(devices):
    me = lax.axis_index("space")
    barrier = pltpu.get_barrier_semaphore()

    def greet(step, carry):
        pl.semaphore_signal(
            barrier,
            inc=1,
            device_id={"space": lax.rem(me + step, devices)},
            device_id_type=pl.DeviceIdType.MESH,
        )
        return carry

    lax.fori_loop(1, devices, greet, 0)


def meet_peers(devices):
    pl.semaphore_wait(pltpu.get_barrier_semaphore(), devices - 1)


def message(devices, channels, src, recv, sems, step, part, owner):
    me = lax.axis_index("space")
    peer = lax.rem(me + step, devices)
    there = pl.ds(pl.multiple_of(peer * channels + part * 8, 8), 8)
    here = pl.ds(pl.multiple_of(owner * channels + part * 8, 8), 8)
    return pltpu.make_async_remote_copy(
        src_ref=src.at[there],
        dst_ref=recv.at[here],
        send_sem=sems.at[0, part, step],
        recv_sem=sems.at[1, part, step],
        device_id={"space": peer},
        device_id_type=pl.DeviceIdType.MESH,
    )


def send_part(devices, channels, src, recv, sems, part):
    me = lax.axis_index("space")

    def send(step, carry):
        message(devices, channels, src, recv, sems, step, part, me).start()
        return carry

    lax.fori_loop(1, devices, send, 0)


def keep_own(channels, src, recv):
    me = lax.axis_index("space")
    own = pl.ds(pl.multiple_of(me * channels, channels), channels)
    recv[own, :] = src[own, :]


def take_part(devices, channels, src, recv, sems, part):
    me = lax.axis_index("space")

    def take(step, carry):
        owner = lax.rem(me + devices - step, devices)
        done = message(devices, channels, src, recv, sems, step, part, owner)
        done.wait_send()
        done.wait_recv()
        return carry

    lax.fori_loop(1, devices, take, 0)


def x_modes(devices, channels, scale, recv, part, real_ref, imag_ref):
    start = pl.multiple_of(part * 8, 8)
    parts = [recv[pl.ds(x * channels + start, 8), :] for x in range(devices)]
    for k, value in enumerate(along_x(parts, 1)):
        value = value * scale
        real, imag = value[:, : 2 * MZ], value[:, 2 * MZ :]
        for alias in range(k, real_ref.shape[0], devices):
            real_ref[alias, pl.ds(start, 8), :] = real
            imag_ref[alias, pl.ds(start, 8), :] = imag


def front_kernel(
    devices, channels, scale, x_ref, tzh, tzl, tyh, tyl, real_ref, imag_ref, lines, src, recv, sems
):
    part = pl.program_id(0)

    @pl.when(part == 0)
    def _():
        greet_peers(devices)

    rows, ny, nz = x_ref.shape
    value = x_ref[...].reshape(rows * ny, nz)
    along = dot3(split(value), (tzh[...], tzl[...]))
    lines[...] = along.reshape(rows, ny, 4 * MZ)
    ty = (tyh[...], tyl[...])
    for c in range(rows):
        src[pl.ds(part * rows + c, devices, stride=channels), :] = message_rows(ty, lines[c])

    @pl.when(part == 0)
    def _():
        meet_peers(devices)

    send_part(devices, channels, src, recv, sems, part)

    @pl.when(part == pl.num_programs(0) - 1)
    def _():
        keep_own(channels, src, recv)

        def finish(part, carry):
            take_part(devices, channels, src, recv, sems, part)
            x_modes(devices, channels, scale, recv, part, real_ref, imag_ref)
            return carry

        lax.fori_loop(0, channels // 8, finish, 0)


def in_hbm(*arrays):
    return [pltpu.with_memory_space_constraint(a, pltpu.HBM) for a in arrays]


def front(field, devices, scale):
    channels, _, ny, nz = field.shape
    tables = packed_tables(ny, nz)
    parts = channels // 8
    spectrum = jax.ShapeDtypeStruct((MX, channels, 2 * MZ), jnp.float32)
    return pl.pallas_call(
        functools.partial(front_kernel, devices, channels, scale),
        grid=(parts,),
        out_shape=(spectrum, spectrum),
        in_specs=[pl.BlockSpec((8, None, ny, nz), lambda c: (c, 0, 0, 0))]
        + [whole(t) for t in tables],
        out_specs=(whole(spectrum), whole(spectrum)),
        scratch_shapes=[
            pltpu.VMEM((8, ny, 4 * MZ), jnp.float32),
            pltpu.VMEM((devices * channels, 4 * MZ), jnp.float32),
            pltpu.VMEM((devices * channels, 4 * MZ), jnp.float32),
            pltpu.SemaphoreType.DMA((2, parts, devices)),
        ],
        compiler_params=pltpu.CompilerParams(
            collective_id=0, has_side_effects=True, vmem_limit_bytes=20 * 2**20
        ),
        name="front",
    )(*in_hbm(field, *tables))


def mix_kernel(devices, channels, real_ref, imag_ref, w_ref, out_ref, both, mixed, src, recv, sems):
    greet_peers(devices)
    local = real_ref.shape[2]
    aliases = range(0, real_ref.shape[0], devices)
    parts = channels // 8
    for k in range(devices):
        both[0, k] = jnp.concatenate([real_ref[k]] * 2, axis=1)
        both[1, k] = jnp.concatenate([imag_ref[k]] * 2, axis=1)

    def one_half(half, carry):
        def one_k(k, inner):
            by_real = [jnp.zeros((8, 2 * local), jnp.float32)] * 2
            by_imag = [jnp.zeros((8, 2 * local), jnp.float32)] * 2
            for i in range(channels):
                real = jnp.broadcast_to(both[0, k, i : i + 1, :], (8, 2 * local))
                imag = jnp.broadcast_to(both[1, k, i : i + 1, :], (8, 2 * local))
                for part in range(2):
                    rows = pl.ds(pl.multiple_of(half * 16 + part * 8, 8), 8)
                    w_real = w_ref[0, k, i, rows, :]
                    w_imag = w_ref[1, k, i, rows, :]
                    for alias in aliases[1:]:
                        w_real = w_real + w_ref[0, k + alias, i, rows, :]
                        w_imag = w_imag + w_ref[1, k + alias, i, rows, :]
                    pair = jnp.concatenate([w_real, w_imag], axis=1)
                    by_real[part] = by_real[part] + real * pair
                    by_imag[part] = by_imag[part] + imag * pair
            for part in range(2):
                mixed[k, part] = by_real[part] - turn(by_imag[part])
            return inner

        lax.fori_loop(0, devices, one_k, 0)

        @pl.when(half == 0)
        def _():
            meet_peers(devices)

        def one_part(part, inner):
            start = pl.multiple_of(half * 16 + part * 8, 8)
            for x, value in enumerate(along_x([mixed[k, part] for k in range(devices)], -1)):
                src[pl.ds(x * channels + start, 8), :] = value
            send_part(devices, channels, src, recv, sems, half * 2 + part)
            return inner

        lax.fori_loop(0, 2, one_part, 0)
        return carry

    lax.fori_loop(0, parts // 2, one_half, 0)
    keep_own(channels, src, recv)

    def finish(part, carry):
        take_part(devices, channels, src, recv, sems, part)
        return carry

    lax.fori_loop(0, parts, finish, 0)
    for quad in range(channels // 4):
        rows = [
            recv[pl.ds(quad * 4 + c, devices, stride=channels), :] for c in range(4)
        ]
        for block in range(4):
            lanes = slice(block * MZ, (block + 1) * MZ)
            out_ref[
                block * devices : (block + 1) * devices, quad * 4 * MZ : (quad + 1) * 4 * MZ
            ] = jnp.concatenate([row[:, lanes] for row in rows], axis=1)


def mix_to_grid(real, imag, weights, devices):
    channels = real.shape[1]
    weights = pltpu.with_memory_space_constraint(weights.transpose(0, 1, 3, 4, 2), pltpu.VMEM)
    out = jax.ShapeDtypeStruct((4 * devices, channels * MZ), jnp.float32)
    vmem = pl.BlockSpec(memory_space=pltpu.VMEM)
    return pl.pallas_call(
        functools.partial(mix_kernel, devices, channels),
        out_shape=out,
        in_specs=[vmem, vmem, vmem],
        out_specs=vmem,
        scratch_shapes=[
            pltpu.VMEM((2, devices, channels, 4 * MZ), jnp.float32),
            pltpu.VMEM((devices, 2, 8, 4 * MZ), jnp.float32),
            pltpu.VMEM((devices * channels, 4 * MZ), jnp.float32),
            pltpu.VMEM((devices * channels, 4 * MZ), jnp.float32),
            pltpu.SemaphoreType.DMA((2, channels // 8, devices)),
        ],
        compiler_params=pltpu.CompilerParams(
            collective_id=1, has_side_effects=True, vmem_limit_bytes=8 * 2**20
        ),
        name="mix",
    )(real, imag, weights)


def middle_packed_kernel(
    devices, m_ref, x_ref, cot_ref, w_ref, bias_ref, pick, bdh, bdl, iyh, iyl, tzh, tzl, tyh, tyl,
    act_ref, modes_ref, point_ref, lines, inverse, field_part, wh, wl, total, bias, point,
):
    step = pl.program_id(1)
    channels, rows, nz = x_ref.shape
    quads = channels // 4
    width = 4 * MZ
    ny = lines.shape[1]

    def same_row():
        size = channels * ROWS
        row = lax.broadcasted_iota(jnp.int32, (size, size), 0) % ROWS
        column = lax.broadcasted_iota(jnp.int32, (size, size), 1) % ROWS
        return row == column

    @pl.when(step == 0)
    def _():
        for part in range(0, m_ref.shape[1], 256):
            lanes = pl.ds(part, 256)
            both = dot3((iyh[...], iyl[...]), split(m_ref[:, lanes]))
            inverse[0, :, lanes] = both[:ny]
            inverse[1, :, lanes] = both[ny:]
        contract = (((1,), (1,)), ((), ()))
        for narrow, out in zip(split(w_ref[...]), (wh, wl)):
            tall = lax.dot_general(
                pick[...], narrow, contract, preferred_element_type=jnp.float32
            ).astype(jnp.bfloat16)
            square = lax.dot_general(tall, pick[...], contract, preferred_element_type=jnp.float32)
            out[...] = jnp.where(same_row(), square, 0.0).astype(jnp.bfloat16)
        total[...] = jnp.zeros_like(total)
        rest = jnp.broadcast_to(bias_ref[...], (nz, channels))
        wide = jnp.zeros_like(bias)
        for _ in range(3):
            narrow = rest.astype(jnp.bfloat16)
            rest = rest - narrow.astype(jnp.float32)
            wide = wide + lax.dot_general(
                pick[...], narrow, contract, preferred_element_type=jnp.float32
            )
        bias[...] = wide

    first = pl.multiple_of(step * rows, rows)
    stacked = jnp.concatenate(
        [
            jnp.concatenate(
                [
                    inverse[r, pl.ds(first, rows), g * width : (g + 1) * width]
                    for r in range(2)
                ],
                axis=1,
            )
            for g in range(quads)
        ],
        axis=0,
    )
    stacked = split(stacked)
    for c in range(4):
        lanes = slice(c * nz, (c + 1) * nz)
        field_part[:, lanes] = dot3(stacked, (bdh[:, lanes], bdl[:, lanes]))

    for half in range(rows // ROWS):
        here = slice(half * ROWS, (half + 1) * ROWS)
        start = pl.multiple_of(step * rows + half * ROWS, ROWS)
        spectral = jnp.concatenate(
            [
                field_part[
                    g * rows + half * ROWS : g * rows + (half + 1) * ROWS, c * nz : (c + 1) * nz
                ]
                for g in range(quads)
                for c in range(4)
            ],
            axis=0,
        )
        field = split(x_ref[:, here, :].reshape(channels * ROWS, nz))
        before = spectral + dot3((wh[...], wl[...]), field)
        before = (before + bias[...]).reshape(channels, ROWS, nz)
        normal = 0.5 * (1.0 + lax.erf(before * INV_SQRT_TWO))
        density = jnp.exp(-0.5 * before * before) * INV_SQRT_TWO_PI
        act_ref[:, here, :] = (before * normal).astype(jnp.bfloat16)
        slope = cot_ref[:, here, :].astype(jnp.float32) * (normal + before * density)
        slope = split(slope.reshape(channels * ROWS, nz))
        total[...] += dot3(field, slope, (((1,), (1,)), ((), ())))
        along = dot3(slope, (tzh[...], tzl[...]))
        lines[:, pl.ds(start, ROWS), :] = along.reshape(channels, ROWS, 4 * MZ)

    @pl.when(step == pl.num_programs(1) - 1)
    def _():
        ty = (tyh[...], tyl[...])

        def finish(c, carry):
            modes_ref[pl.ds(c, devices, stride=channels), :] = message_rows(ty, lines[c])
            return carry

        lax.fori_loop(0, channels, finish, 0, unroll=8)
        diagonal = jnp.where(same_row(), total[...], 0.0)
        rows_sum = jnp.sum(diagonal.reshape(channels, ROWS, channels * ROWS), axis=1)
        high, low = split(rows_sum)
        folded = jnp.dot(high, pick[...], preferred_element_type=jnp.float32) + jnp.dot(
            low, pick[...], preferred_element_type=jnp.float32
        )
        own_bias = modes_ref[:channels, :channels]
        lane = lax.broadcasted_iota(jnp.int32, (channels, channels), 1)
        own_bias = jnp.where(lane == 0, own_bias, 0.0)
        spare = jnp.zeros((channels, 4 * MZ - 2 * channels), jnp.float32)
        point[...] = jnp.concatenate([folded, own_bias, spare], axis=1)
        first_rows = point[pl.ds(0, channels // 2, stride=2), :]
        second_rows = point[pl.ds(1, channels // 2, stride=2), :]
        packed = first_rows + pltpu.roll(second_rows, 2 * MZ, 1)
        for d in range(channels // 2):
            point_ref[d] = packed[d : d + 1]


def middle_packed(grid_modes, devices, field, cotangent, point_weights, point_bias, scale):
    channels, width, ny, nz = field.shape
    size = channels * ROWS
    tables = inverse_tables(ny, nz, scale, None) + packed_tables(ny, nz)
    pick = jnp.asarray(np.repeat(np.eye(channels, dtype=np.float32), ROWS, 0).astype(jnp.bfloat16))
    bias = point_bias.reshape(1, channels)
    spec = field_spec(channels, nz)
    mixed_spec = pl.BlockSpec((None,) + grid_modes.shape[1:], lambda x, y: (x, 0, 0))
    return pl.pallas_call(
        functools.partial(middle_packed_kernel, devices),
        grid=(width, ny // STEP),
        out_shape=(
            jax.ShapeDtypeStruct(field.shape, jnp.bfloat16),
            jax.ShapeDtypeStruct((devices * channels, 4 * MZ), jnp.float32),
            jax.ShapeDtypeStruct((channels // 2, 1, 4 * MZ), jnp.float32),
        ),
        in_specs=[mixed_spec, spec, spec, whole(point_weights), whole(bias), whole(pick)]
        + [whole(t) for t in tables],
        out_specs=(
            spec,
            pl.BlockSpec((devices * channels, 4 * MZ), lambda x, y: (0, 0)),
            pl.BlockSpec((channels // 2, 1, 4 * MZ), lambda x, y: (0, 0, 0)),
        ),
        scratch_shapes=[
            pltpu.VMEM((channels, ny, 4 * MZ), jnp.float32),
            pltpu.VMEM((2, ny, channels * MZ), jnp.float32),
            pltpu.VMEM((channels // 4 * STEP, 4 * nz), jnp.float32),
            pltpu.VMEM((size, size), jnp.bfloat16),
            pltpu.VMEM((size, size), jnp.bfloat16),
            pltpu.VMEM((size, size), jnp.float32),
            pltpu.VMEM((size, nz), jnp.float32),
            pltpu.VMEM((channels, 4 * MZ), jnp.float32),
        ],
        compiler_params=pltpu.CompilerParams(vmem_limit_bytes=28 * 2**20),
        name="middle_packed",
    )(grid_modes, *in_hbm(field, cotangent, point_weights, bias, pick, *tables))


def tail_kernel(
    devices, channels, scale, src, point_ref, slope_ref, turned_ref, sums_ref, bias_ref,
    recv, partial, total, gathered, sems, point_sems,
):
    me = lax.axis_index("space")
    greet_peers(devices)
    meet_peers(devices)

    def point_message(step, phase, source, target):
        peer = lax.rem(me + step, devices)
        return pltpu.make_async_remote_copy(
            src_ref=source(peer),
            dst_ref=target,
            send_sem=point_sems.at[phase, 0, step],
            recv_sem=point_sems.at[phase, 1, step],
            device_id={"space": peer},
            device_id_type=pl.DeviceIdType.MESH,
        )

    def scatter(step, owner):
        return point_message(step, 0, lambda peer: point_ref.at[peer], partial.at[owner])

    def gather(step, owner):
        return point_message(step, 1, lambda peer: total, gathered.at[owner])

    def start(make):
        def one(step, carry):
            make(step, me).start()
            return carry

        lax.fori_loop(1, devices, one, 0)

    def finish(make):
        def one(step, carry):
            done = make(step, lax.rem(me + devices - step, devices))
            done.wait_send()
            done.wait_recv()
            return carry

        lax.fori_loop(1, devices, one, 0)

    start(scatter)
    for part in range(channels // 8):
        send_part(devices, channels, src, recv, sems, part)
    keep_own(channels, src, recv)
    partial[me] = point_ref[me]
    finish(scatter)
    summed = partial[0]
    for d in range(1, devices):
        summed = summed + partial[d]
    total[...] = summed * scale
    start(gather)
    gathered[me] = total[...]
    weight = jnp.where(lane_ids(8) % MZ == 0, scale, 2.0 * scale)

    def one_part(part, carry):
        take_part(devices, channels, src, recv, sems, part)
        first = pl.multiple_of(part * 8, 8)
        rows = pl.ds(first, 8)
        parts = [recv[pl.ds(x * channels + first, 8), :] for x in range(devices)]
        for k, value in enumerate(along_x(parts, 1)):
            value = value * weight
            real, imag = value[:, : 2 * MZ], value[:, 2 * MZ :]
            for alias in range(k, slope_ref.shape[1], devices):
                slope_ref[0, alias, rows, :] = real
                slope_ref[1, alias, rows, :] = imag
                turned_ref[0, alias, rows, :] = imag
                turned_ref[1, alias, rows, :] = -real
        return carry

    lax.fori_loop(0, channels // 8, one_part, 0)
    finish(gather)
    for d in range(devices):
        row = gathered[d]
        both = jnp.concatenate([row[:, : 2 * MZ], row[:, 2 * MZ :]], axis=0)
        sums_ref[2 * d : 2 * d + 2, :] = both[:, :channels]
        bias_ref[2 * d : 2 * d + 2, :] = both[:, channels : channels + 1]


def tail(modes, point, devices, scale):
    channels = modes.shape[0] // devices
    parts = channels // 8
    vmem = pl.BlockSpec(memory_space=pltpu.VMEM)
    slope = jax.ShapeDtypeStruct((2, MX, channels, 2 * MZ), jnp.float32)
    return pl.pallas_call(
        functools.partial(tail_kernel, devices, channels, scale),
        out_shape=(
            slope,
            slope,
            jax.ShapeDtypeStruct((channels, channels), jnp.float32),
            jax.ShapeDtypeStruct((channels, 1), jnp.float32),
        ),
        in_specs=[vmem] * 2,
        out_specs=(vmem,) * 4,
        scratch_shapes=[
            pltpu.VMEM((devices * channels, 4 * MZ), jnp.float32),
            pltpu.VMEM((devices, 1, 4 * MZ), jnp.float32),
            pltpu.VMEM((1, 4 * MZ), jnp.float32),
            pltpu.VMEM((devices, 1, 4 * MZ), jnp.float32),
            pltpu.SemaphoreType.DMA((2, parts, devices)),
            pltpu.SemaphoreType.DMA((2, 2, devices)),
        ],
        compiler_params=pltpu.CompilerParams(collective_id=2, has_side_effects=True, vmem_limit_bytes=8 * 2**20),
        name="tail",
    )(modes, point)


def x_table(length_x):
    return angles(np.arange(length_x), kept(MX, length_x), length_x)


def exchange_kernel(devices, src, out, send_sem, recv_sem, own_sem):
    me = lax.axis_index("space")
    barrier = pltpu.get_barrier_semaphore()

    def greet(step, carry):
        peer = lax.rem(me + step, devices)
        pl.semaphore_signal(
            barrier, inc=1, device_id={"space": peer}, device_id_type=pl.DeviceIdType.MESH
        )
        return carry

    def copy(step, slot):
        peer = lax.rem(me + step, devices)
        return pltpu.make_async_remote_copy(
            src_ref=src.at[peer],
            dst_ref=out.at[slot],
            send_sem=send_sem.at[step],
            recv_sem=recv_sem.at[step],
            device_id={"space": peer},
            device_id_type=pl.DeviceIdType.MESH,
        )

    def send(step, carry):
        copy(step, me).start()
        return carry

    def finish(step, carry):
        done = copy(step, lax.rem(me + devices - step, devices))
        done.wait_send()
        done.wait_recv()
        return carry

    lax.fori_loop(1, devices, greet, 0)
    own = pltpu.make_async_copy(src.at[me], out.at[me], own_sem)
    own.start()
    pl.semaphore_wait(barrier, devices - 1)
    lax.fori_loop(1, devices, send, 0)
    own.wait()
    lax.fori_loop(1, devices, finish, 0)


def exchange(lines, identity):
    devices = lax.axis_size("space")
    shape = lines.shape
    lines = lines.reshape(devices, -1, 128)
    vmem = pl.BlockSpec(memory_space=pltpu.VMEM)
    out = pl.pallas_call(
        functools.partial(exchange_kernel, devices),
        out_shape=jax.ShapeDtypeStruct(lines.shape, jnp.float32),
        in_specs=[vmem],
        out_specs=vmem,
        scratch_shapes=[
            pltpu.SemaphoreType.DMA((devices,)),
            pltpu.SemaphoreType.DMA((devices,)),
            pltpu.SemaphoreType.DMA,
        ],
        compiler_params=pltpu.CompilerParams(collective_id=identity, has_side_effects=True),
        name=f"exchange_{identity}",
    )(lines)
    return out.reshape(shape)


def to_spectrum(modes, scale, devices, extra=None):
    width, channels = modes.shape[:2]
    local = MY * MZ // devices
    lines = modes.reshape(width, channels, MY, 2, MZ).transpose(0, 3, 1, 2, 4)
    lines = lines.reshape(width, 2, channels, devices, local).transpose(3, 0, 1, 2, 4)
    lines = lines.reshape(devices, width * 2 * channels * local)
    size = lines.shape[1]
    if extra is not None:
        extra = jnp.pad(extra, (0, -extra.shape[0] % 128))
        extra = jnp.broadcast_to(extra[None], (devices,) + extra.shape)
        lines = jnp.concatenate([lines, extra], axis=1)
    lines = exchange(lines, 0 if extra is None else 2)
    summed = jnp.sum(lines[:, size:], axis=0)
    lines = lines[:, :size].reshape(devices * width, 2, channels, local)
    cos_x, sin_x = x_table(devices * width)
    table = np.stack([np.stack([cos_x, -sin_x], 1), np.stack([sin_x, cos_x], 1)], 1)
    table = jnp.asarray((table * scale).astype(np.float32))
    return jnp.einsum("xrcm,xrqk->qkcm", lines, table, precision=HIGH), summed


def mix_modes(spectrum, weights):
    real, imag = spectrum[0], spectrum[1]
    out_real = jnp.einsum("kim,kmio->kom", real, weights[0], precision=HIGH) - jnp.einsum(
        "kim,kmio->kom", imag, weights[1], precision=HIGH
    )
    out_imag = jnp.einsum("kim,kmio->kom", real, weights[1], precision=HIGH) + jnp.einsum(
        "kim,kmio->kom", imag, weights[0], precision=HIGH
    )
    return jnp.stack([out_real, out_imag], axis=0)


def to_grid(mixed, length_x):
    channels = mixed.shape[2]
    cos_x, sin_x = x_table(length_x)
    table = np.stack([np.stack([cos_x, sin_x], 0), np.stack([-sin_x, cos_x], 0)], 0)
    table = jnp.asarray(table.astype(np.float32))
    lines = jnp.einsum("rkom,rqxk->xqom", mixed, table, precision=HIGH)
    local = mixed.shape[3]
    devices = MY * MZ // local
    width = length_x // devices
    if local % MZ == 0:
        local_rows = local // MZ
        lines = lines.reshape(length_x, 2, channels, local_rows, MZ).transpose(0, 1, 3, 2, 4)
        lines = exchange(lines.reshape(length_x, 2 * local_rows * channels * MZ), 1)
        grid = lines.reshape(devices, width, 2 * local_rows, channels * MZ).transpose(1, 0, 2, 3)
    else:
        local_rows = 1
        lines = exchange(lines.reshape(length_x, 2 * channels * local), 1)
        grid = lines.reshape(MY, MZ // local, width, 2, channels, local).transpose(2, 0, 3, 4, 1, 5)
    return grid.reshape(width, 2 * MY, channels * MZ), local_rows


def body(lifted_field, cotangent, spectral_weights, point_weights, point_bias):
    devices = lax.axis_size("space")
    channels, width, ny, nz = lifted_field.shape
    length_x = width * devices
    scale = 1.0 / float(length_x * ny * nz) ** 0.5
    packed = width == 1 and MY == 2 * devices == channels and MX % devices == 0
    if packed:
        real, imag = front(lifted_field, devices, scale)
        grid_modes = mix_to_grid(real, imag, spectral_weights, devices)[None]
        activated, modes, point = middle_packed(
            grid_modes, devices, lifted_field, cotangent, point_weights, point_bias, scale
        )
        slope, turned, summed_point, summed_bias = tail(modes, point, devices, scale)
        grad_spectral = real[None, :, :, None] * slope[:, :, None] + imag[None, :, :, None] * turned[:, :, None]
        return (
            activated,
            grad_spectral.transpose(0, 1, 4, 2, 3),
            summed_point,
            summed_bias.reshape(-1),
        )
    else:
        spectrum, _ = to_spectrum(forward_modes(lifted_field), scale, devices)
        grid_modes, local_rows = to_grid(mix_modes(spectrum, spectral_weights), length_x)
    activated, slope_modes, wide_point = middle(
        grid_modes, local_rows, lifted_field, cotangent, point_weights, point_bias, scale
    )
    local_point = jnp.sum(wide_point.reshape(width, channels, channels, ROWS), axis=(0, 3))
    local_bias = jnp.sum(slope_modes[:, :, 0, 0], axis=0)
    partial = jnp.concatenate([local_point.reshape(-1), local_bias])
    slope_spectrum, summed = to_spectrum(slope_modes, scale, devices, partial)
    area = channels * channels
    summed_point = summed[:area].reshape(channels, channels)
    summed_bias = summed[area : area + channels]
    local_modes = spectrum.shape[3]
    mode_ids = lax.axis_index("space") * local_modes + jnp.arange(local_modes, dtype=jnp.int32)
    weight_modes = jnp.where(mode_ids % MZ == 0, 1.0, 2.0).astype(jnp.float32)
    grad_spectral = weight_gradient(spectrum, slope_spectrum * weight_modes)
    return (activated, grad_spectral, summed_point * scale, summed_bias * scale)


def solution(mesh):
    placed = (
        P("groups", "space", None, None),
        P("groups", "space", None, None),
        P(None, None, "space", None, None),
        P(),
        P(),
    )
    return jax.shard_map(
        body,
        mesh=mesh,
        in_specs=placed,
        out_specs=(
            P("groups", "space", None, None),
            P("groups", None, "space", None, None),
            P("groups", None),
            P("groups"),
        ),
        check_vma=False,
    )
```
